512 devices in a mesh: dp: 16 (over x, y), expert: 32 (over z, core).
Axes of the slice: x: 4, y: 4, z: 16, core: 2. Of those that a mesh axis runs over, the one named last changes fastest.
Arguments:
- tokens: bfloat16 [16384, 3584], P('expert', 'dp'), may hold values from -6 to 6
- grad_out: bfloat16 [16384, 3584], P('expert', 'dp'), may hold values from -1.796875 to 1.796875
- expert_ids: int32 [16384, 8], P('expert'), may hold values from 0 to 255, as said below
- gates: float32 [16384, 8], P('expert'), may hold values from 0.25 to 2.5
- w_gate: bfloat16 [32, 3584, 1024], P('expert', 'dp'), may hold values from -0.09375 to 0.09375
- w_up: bfloat16 [32, 3584, 1024], P('expert', 'dp'), may hold values from -0.09375 to 0.09375
- w_down: bfloat16 [32, 1024, 3584], P('expert', None, 'dp'), may hold values from -0.1875 to 0.1875
Outputs:
- mixed: bfloat16 [16384, 3584], P('expert', 'dp')
- grad_tokens: bfloat16 [16384, 3584], P('expert', 'dp')
- grad_gate: bfloat16 [32, 3584, 1024], P('expert', 'dp')
- grad_up: bfloat16 [32, 3584, 1024], P('expert', 'dp')
- grad_down: bfloat16 [32, 1024, 3584], P('expert', None, 'dp')
The draws below stay inside these ranges and needn't reach their ends.
Inputs may be any that keep to these rules, and one draw needn't show every extreme that they name: `expert_ids`: each row names 8 different experts, at most one of them below 32. Within each aligned block of 512 rows no expert below 32 is named by more than 32 rows, and one such expert, the same in every block, is named by exactly 32 rows of every block.
All inputs are finite; a program needn't handle non-finite values.
Results may differ from the reference program's by a relative error of at most 0.029.
Values may be sent and summed in bfloat16 or wider, within the bound.
A program may use at most 64 MiB of HBM per device.

```python
import math
import jax
import jax.numpy as jnp
from jax import lax

D = 3584
HID = 1024
N_ROUTED = 256
TOPK = 8
TOK_E = 512
CAP = 32
EXPERTS = 32
TOKENS = 16384
SLOTS = 1024
FEAT_DEV = 224
N_DP = 16


def draw_expert_ids(key, part):
    key_hot, key_pref, key_blocks = jax.random.split(key, 3)
    hot_expert = jax.random.randint(key_hot, (), 0, EXPERTS)
    preference = jax.random.permutation(key_pref, EXPERTS)
    spread = (N_ROUTED - EXPERTS) // TOPK

    def one_block(block_key):
        key_order, key_first, key_second, key_drop, key_base, key_place = jax.random.split(block_key, 6)
        shuffled = jax.random.permutation(key_order, TOK_E)
        is_hot = shuffled < CAP
        first_draw = jax.random.randint(key_first, (TOK_E,), 0, EXPERTS)
        second_draw = jax.random.randint(key_second, (TOK_E,), 0, EXPERTS)
        chosen = preference[jnp.minimum(first_draw, second_draw)]
        chosen = jnp.where(is_hot, hot_expert, chosen)
        one_hot = (chosen[:, None] == jnp.arange(EXPERTS)[None, :]).astype(jnp.int32)
        position = jnp.sum((jnp.cumsum(one_hot, axis=0) - one_hot) * one_hot, axis=1)
        dropped = jax.random.randint(key_drop, (TOK_E,), 0, 8) == 0
        kept_pick = is_hot | (chosen != hot_expert) & (position < CAP) & jnp.logical_not(dropped)
        offset_base = jax.random.randint(key_base, (TOK_E,), 0, spread)
        outside = EXPERTS + offset_base[:, None] + spread * jnp.arange(TOPK)[None, :]
        place_index = jax.random.randint(key_place, (TOK_E,), 0, TOPK)
        at_place = jnp.arange(TOPK)[None, :] == place_index[:, None]
        return jnp.where(at_place & kept_pick[:, None], chosen[:, None], outside).astype(jnp.int32)
    block_keys = jax.random.split(key_blocks, TOKENS // TOK_E)
    return jax.vmap(one_block)(block_keys).reshape(TOKENS, TOPK)


def block_levels(own_key, extent, cuts, low, high):
    def one(axis_at, parts):
        draws = jax.random.uniform(jax.random.fold_in(jax.random.fold_in(own_key, 6), axis_at), (parts,), jnp.float32, low / len(cuts), high / len(cuts))
        return jnp.repeat(jnp.exp(draws), extent[axis_at] // parts).reshape((-1,) + (1,) * (len(extent) - axis_at - 1))

    gain = one(*cuts[0])
    for cut in cuts[1:]:
        gain = gain * one(*cut)
    return gain


def scatter_about(stream_key, extent, deviation, limit, cuts=(), held_as=jnp.bfloat16):
    gain = block_levels(stream_key, extent, cuts, -0.22, 0.18) if cuts else 1.0
    result = jax.random.normal(stream_key, extent, jnp.float32) * deviation * gain
    return jnp.minimum(jnp.maximum(result, -limit), limit).astype(held_as)


def setup_inputs(seed: int = 0) -> dict:
    seeds = jax.random.split(jax.random.key(seed), 8)
    return {
        "tokens": scatter_about(seeds[0], (TOKENS, D), 1.0, 6.0, ((0, 32), (1, 16))),
        "grad_out": scatter_about(seeds[1], (TOKENS, D), 0.3, 1.796875, ((0, 32), (1, 16))),
        "expert_ids": draw_expert_ids(jax.random.fold_in(seeds[7], 71), 0),
        "gates": jnp.clip(jnp.exp(math.log(2.5) - 2.3025851 * jax.random.uniform(seeds[3], (TOKENS, TOPK), jnp.float32) ** block_levels(seeds[3], (TOKENS, TOPK), ((0, 32),), -0.2, 0.2)), 0.25, 2.5),
        "w_gate": scatter_about(seeds[4], (EXPERTS, D, HID), D ** -0.5, 0.09375, ((0, 32), (1, 16))),
        "w_up": scatter_about(seeds[5], (EXPERTS, D, HID), D ** -0.5, 0.09375, ((0, 32), (1, 16))),
        "w_down": scatter_about(seeds[6], (EXPERTS, HID, D), HID ** -0.5, 0.1875, ((0, 32), (2, 16))),
    }


def swish_gate(value):
    return value * jax.nn.sigmoid(value)


def swish_slope(value):
    logistic = jax.nn.sigmoid(value)
    return logistic * (1.0 + value * (1.0 - logistic))


def grouped_rounded_sum(partial_terms):
    rounded = lax.optimization_barrier(partial_terms.astype(jnp.bfloat16))
    return jnp.sum(rounded.astype(jnp.float32), axis=0)


def reference(tokens, grad_out, expert_ids, gates, w_gate, w_up, w_down):
    in_window = expert_ids < EXPERTS
    routed = jnp.any(in_window, axis=1)
    chosen = jnp.sum(jnp.where(in_window, expert_ids, 0), axis=1).astype(jnp.int32)
    weight_tok = jnp.sum(jnp.where(in_window, gates, jnp.zeros_like(gates)), axis=1)
    one_hot = ((chosen[:, None] == jnp.arange(EXPERTS, dtype=jnp.int32)[None, :]) & routed[:, None]).astype(jnp.int32)
    one_hot = one_hot.reshape(TOKENS // TOK_E, TOK_E, EXPERTS)
    position = jnp.sum((jnp.cumsum(one_hot, axis=1) - one_hot) * one_hot, axis=2).reshape(TOKENS).astype(jnp.int32)
    slot_index = (jnp.arange(TOKENS, dtype=jnp.int32) // TOK_E) * CAP + position
    flat_index = jnp.where(routed, chosen * SLOTS + slot_index, EXPERTS * SLOTS).astype(jnp.int32)
    row_table = jnp.full((EXPERTS * SLOTS,), TOKENS, jnp.int32)
    row_table = row_table.at[flat_index].set(jnp.arange(TOKENS, dtype=jnp.int32), mode="drop").reshape(EXPERTS, SLOTS)
    scaled = (weight_tok[:, None] * grad_out.astype(jnp.float32)).astype(jnp.bfloat16)

    def per_expert(pieces):
        table_rows, gate_mat, up_mat, down_mat = pieces
        expert_rows = jnp.take(tokens, table_rows, axis=0, mode="fill", fill_value=0)
        grad_rows_in = jnp.take(scaled, table_rows, axis=0, mode="fill", fill_value=0)
        grouped_rows = expert_rows.reshape(SLOTS, N_DP, FEAT_DEV).astype(jnp.float32)
        gate_groups = gate_mat.reshape(N_DP, FEAT_DEV, HID).astype(jnp.float32)
        up_groups = up_mat.reshape(N_DP, FEAT_DEV, HID).astype(jnp.float32)
        gate_pre = grouped_rounded_sum(jnp.einsum("snf,nfh->nsh", grouped_rows, gate_groups))
        up_pre = grouped_rounded_sum(jnp.einsum("snf,nfh->nsh", grouped_rows, up_groups))
        activation = (swish_gate(gate_pre) * up_pre).astype(jnp.bfloat16)
        expert_out = jnp.dot(activation, down_mat, preferred_element_type=jnp.float32).astype(jnp.bfloat16)
        grad_down = jnp.dot(activation.T, grad_rows_in, preferred_element_type=jnp.float32).astype(jnp.bfloat16)
        grouped_grads = grad_rows_in.reshape(SLOTS, N_DP, FEAT_DEV).astype(jnp.float32)
        down_groups = down_mat.reshape(HID, N_DP, FEAT_DEV).astype(jnp.float32)
        grad_act = grouped_rounded_sum(jnp.einsum("snf,hnf->nsh", grouped_grads, down_groups))
        grad_gate_pre = (grad_act * up_pre * swish_slope(gate_pre)).astype(jnp.bfloat16)
        grad_up_pre = (grad_act * swish_gate(gate_pre)).astype(jnp.bfloat16)
        grad_gate = jnp.dot(expert_rows.T, grad_gate_pre, preferred_element_type=jnp.float32).astype(jnp.bfloat16)
        grad_up = jnp.dot(expert_rows.T, grad_up_pre, preferred_element_type=jnp.float32).astype(jnp.bfloat16)
        row_grad = (jnp.dot(grad_gate_pre, gate_mat.T, preferred_element_type=jnp.float32)
                    + jnp.dot(grad_up_pre, up_mat.T, preferred_element_type=jnp.float32)).astype(jnp.bfloat16)
        return expert_out, row_grad, grad_gate, grad_up, grad_down

    expert_out, row_grad, grad_gate, grad_up, grad_down = lax.map(per_expert, (row_table, w_gate, w_up, w_down))
    token_out = jnp.take(expert_out.reshape(EXPERTS * SLOTS, D), flat_index, axis=0, mode="fill", fill_value=0)
    mixed = (weight_tok[:, None] * token_out.astype(jnp.float32)).astype(jnp.bfloat16)
    grad_tokens = jnp.take(row_grad.reshape(EXPERTS * SLOTS, D), flat_index, axis=0, mode="fill", fill_value=0)
    return (mixed, grad_tokens, grad_gate, grad_up, grad_down)
```

```python
import functools

import jax
import jax.numpy as jnp
from jax import lax
from jax.experimental import pallas as pl
from jax.experimental.pallas import tpu as pltpu
from jax.sharding import PartitionSpec as P

MESH = pl.DeviceIdType.MESH
BF16 = jnp.bfloat16
F32 = jnp.float32
RING = 4
LAG = 3


def dot(left, right, dims):
    return lax.dot_general(left, right, (dims, ((), ())), preferred_element_type=F32)


def wait_bytes(ref, sem):
    pltpu.make_async_copy(ref, ref, sem).wait()


def kernel(
    experts,
    cap,
    chunks,
    tok_ref,
    gout_ref,
    ids_ref,
    gates_ref,
    wg_ref,
    wu_ref,
    wd_ref,
    mixed_ref,
    gtok_ref,
    ggate_ref,
    gup_ref,
    gdown_ref,
    send,
    recv,
    part,
    ra1,
    rb1,
    red,
    ra2,
    rb2,
    full,
    ret,
    back,
    pick,
    acc_g,
    acc_u,
    acc_d,
    disp_send,
    disp_recv,
    back_send,
    back_recv,
    xy_send,
    ra1_sem,
    rb1_sem,
    ra2_sem,
    rb2_sem,
    ag2_sem,
    ag1_sem,
):
    dp = lax.axis_index("dp")
    me = lax.axis_index("expert")
    px, py = dp // RING, dp % RING
    zs = experts // 2
    z, core = me // 2, me % 2
    per = zs // chunks
    blocks = 2 * per
    rows = blocks * cap
    toks, feat = tok_ref.shape
    slots = experts * cap
    col = part.shape[-1]
    q2 = red.shape[-2]

    def peer(dz, dc):
        return ((z + dz) % zs) * 2 + (core if dc == 0 else 1 - core)

    def x_peer(step):
        return ((px + step) % RING) * RING + py

    def y_peer(step):
        return px * RING + (py + step) % RING

    barrier = pltpu.get_barrier_semaphore()
    for dz in range(zs):
        for dc in range(2):
            if dz or dc:
                pl.semaphore_signal(
                    barrier, inc=1, device_id=(dp, peer(dz, dc)), device_id_type=MESH
                )
    for near in (x_peer(1), x_peer(RING - 1), y_peer(1), y_peer(RING - 1)):
        pl.semaphore_signal(barrier, inc=1, device_id=(near, me), device_id_type=MESH)

    ids = ids_ref[...]
    inside = ids < experts
    chosen = jnp.sum(jnp.where(inside, ids, 0).astype(F32), axis=1, keepdims=True)
    routed = jnp.sum(jnp.where(inside, 1.0, 0.0), axis=1, keepdims=True)
    weight = jnp.sum(jnp.where(inside, gates_ref[...], 0.0), axis=1, keepdims=True)
    lane_e = lax.broadcasted_iota(jnp.int32, (toks, experts), 1).astype(F32)
    one_hot = jnp.where((lane_e == chosen) & (routed > 0.0), 1.0, 0.0)
    earlier = jnp.where(
        lax.broadcasted_iota(jnp.int32, (toks, toks), 1)
        < lax.broadcasted_iota(jnp.int32, (toks, toks), 0),
        1.0,
        0.0,
    ).astype(BF16)
    counts = dot(earlier, one_hot.astype(BF16), ((1,), (0,)))
    position = jnp.sum(counts * one_hot, axis=1, keepdims=True)
    slot = jnp.where(routed > 0.0, chosen * cap + position, 2.0 * slots)
    lane_s = lax.broadcasted_iota(jnp.int32, (toks, slots), 1).astype(F32)
    pick[...] = jnp.where(lane_s == slot, 1.0, 0.0).astype(BF16)
    slot_row = jnp.broadcast_to(slot, (toks, 128)).T[0:1, :]
    sub_s = lax.broadcasted_iota(jnp.int32, (slots, toks), 0).astype(F32)
    place = jnp.where(sub_s == slot_row, 1.0, 0.0).astype(BF16)
    scaled = (weight * gout_ref[...].astype(F32)).astype(BF16)
    send[:, 0:cap, :] = (
        dot(place, tok_ref[...], ((1,), (0,))).astype(BF16).reshape(experts, cap, feat)
    )
    send[:, cap : 2 * cap, :] = (
        dot(place, scaled, ((1,), (0,))).astype(BF16).reshape(experts, cap, feat)
    )

    pl.semaphore_wait(barrier, 2 * zs - 1 + 4)

    for c in range(chunks):
        for j in range(per):
            for dc in range(2):
                dz = chunks * j + c
                target = recv.at[c, 2 * j + dc]
                if dz == 0 and dc == 0:
                    pltpu.make_async_copy(send.at[me], target, disp_recv.at[c]).start()
                else:
                    there = peer(zs - dz, dc)
                    pltpu.make_async_remote_copy(
                        src_ref=send.at[there],
                        dst_ref=target,
                        send_sem=disp_send,
                        recv_sem=disp_recv.at[c],
                        device_id=(dp, there),
                        device_id_type=MESH,
                    ).start()

    acc_g[...] = jnp.zeros_like(acc_g)
    acc_u[...] = jnp.zeros_like(acc_u)
    acc_d[...] = jnp.zeros_like(acc_d)

    def hop(src, dst, send_sem, recv_sem, near):
        pltpu.make_async_remote_copy(
            src_ref=src,
            dst_ref=dst,
            send_sem=send_sem,
            recv_sem=recv_sem,
            device_id=(near, me),
            device_id_type=MESH,
        ).start()

    first = ((px, x_peer(1), x_peer(RING - 1)), (py, y_peer(1), y_peer(RING - 1)))
    second = (first[1], first[0])

    def rs_start(src, ra, rb, c, h, ring, ssem, ra_sem, rb_sem):
        p, right, left = ring
        lo, hi = 2 * h, 2 * h + 1
        hop(src.at[c, lo, (p + 2) % 4], ra.at[c, h, 0], ssem, ra_sem.at[c, h, 0], right)
        hop(src.at[c, hi, (p + 2) % 4], ra.at[c, h, 1], ssem, ra_sem.at[c, h, 1], left)
        hop(src.at[c, hi, (p + 1) % 4], rb.at[c, h, 0], ssem, rb_sem.at[c, h], right)
        hop(src.at[c, lo, (p + 3) % 4], rb.at[c, h, 1], ssem, rb_sem.at[c, h], left)

    def rs_relay(src, ra, rb, c, h, ring, ssem, ra_sem, rb_sem):
        p, right, left = ring
        for side, b, t, near in ((0, 2 * h, (p + 1) % 4, right), (1, 2 * h + 1, (p + 3) % 4, left)):
            wait_bytes(ra.at[c, h, side], ra_sem.at[c, h, side])
            src[c, b, t] = (src[c, b, t].astype(F32) + ra[c, h, side].astype(F32)).astype(BF16)
            hop(src.at[c, b, t], rb.at[c, h, 2 + side], ssem, rb_sem.at[c, h], near)

    def rs_final(src, rb, c, h, ring, rb_sem):
        p = ring[0]
        wait_bytes(rb.at[c, h], rb_sem.at[c, h])
        lo = src[c, 2 * h, p].astype(F32) + rb[c, h, 1].astype(F32) + rb[c, h, 2].astype(F32)
        hi = src[c, 2 * h + 1, p].astype(F32) + rb[c, h, 0].astype(F32) + rb[c, h, 3].astype(F32)
        return lo, hi

    def stage_partials(c):
        wait_bytes(recv.at[c], disp_recv.at[c])
        x = recv[c, :, 0:cap, :].reshape(rows, feat)
        g = recv[c, :, cap : 2 * cap, :].reshape(rows, feat)
        for h in range(2):
            for b in (2 * h, 2 * h + 1):
                cols = slice(b * col, (b + 1) * col)
                terms = (
                    dot(x, wg_ref[:, cols], ((1,), (0,))),
                    dot(x, wu_ref[:, cols], ((1,), (0,))),
                    dot(g, wd_ref[cols, :], ((1,), (1,))),
                )
                for a in range(3):
                    part[c, b, :, a] = terms[a].astype(BF16).reshape(4, rows // 4, col)
            rs_start(part, ra1, rb1, c, h, first[h], xy_send.at[c, 0], ra1_sem, rb1_sem)

    def stage_relay1(c):
        for h in range(2):
            rs_relay(part, ra1, rb1, c, h, first[h], xy_send.at[c, 0], ra1_sem, rb1_sem)

    def stage_second(c):
        for h in range(2):
            sums = rs_final(part, rb1, c, h, first[h], rb1_sem)
            for side in range(2):
                for a in range(3):
                    red[c, 2 * h + side, :, a] = sums[side][a].astype(BF16).reshape(4, q2, col)
            rs_start(red, ra2, rb2, c, h, second[h], xy_send.at[c, 1], ra2_sem, rb2_sem)

    def stage_relay2(c):
        for h in range(2):
            rs_relay(red, ra2, rb2, c, h, second[h], xy_send.at[c, 1], ra2_sem, rb2_sem)

    def stage_pointwise(c):
        for h in range(2):
            p1 = first[h][0]
            p2, right, left = second[h]
            sums = rs_final(red, rb2, c, h, second[h], rb2_sem)
            for side in range(2):
                gate, up, grad = sums[side][0], sums[side][1], sums[side][2]
                logistic = 1.0 / (1.0 + jnp.exp(-gate))
                swish = gate * logistic
                full[c, h, p1, p2, side, 0] = (swish * up).astype(BF16)
                full[c, h, p1, p2, side, 1] = (
                    grad * up * (logistic * (1.0 + gate * (1.0 - logistic)))
                ).astype(BF16)
                full[c, h, p1, p2, side, 2] = (grad * swish).astype(BF16)
            own = full.at[c, h, p1, p2]
            hop(own, own, xy_send.at[c, 2], ag2_sem.at[c, h, 0], right)
            hop(own, own, xy_send.at[c, 2], ag2_sem.at[c, h, 1], left)

    def stage_forward2(c):
        for h in range(2):
            p1 = first[h][0]
            p2, right, left = second[h]
            for side, t, near in ((0, (p2 + 3) % 4, right), (1, (p2 + 1) % 4, left)):
                wait_bytes(full.at[c, h, p1, t], ag2_sem.at[c, h, side])
                piece = full.at[c, h, p1, t, side]
                hop(piece, piece, xy_send.at[c, 2], ag2_sem.at[c, h, 2], near)

    def stage_first(c):
        for h in range(2):
            p1, right, left = first[h]
            p2 = second[h][0]
            wait_bytes(full.at[c, h, p1, (p2 + 2) % 4], ag2_sem.at[c, h, 2])
            own = full.at[c, h, p1]
            hop(own, own, xy_send.at[c, 3], ag1_sem.at[c, h, 0], right)
            hop(own, own, xy_send.at[c, 3], ag1_sem.at[c, h, 1], left)

    def stage_forward1(c):
        for h in range(2):
            p1, right, left = first[h]
            for side, t, near in ((0, (p1 + 3) % 4, right), (1, (p1 + 1) % 4, left)):
                wait_bytes(full.at[c, h, t], ag1_sem.at[c, h, side])
                piece = full.at[c, h, t, :, side]
                hop(piece, piece, xy_send.at[c, 3], ag1_sem.at[c, h, 2], near)

    def stage_outputs(c):
        for h in range(2):
            wait_bytes(full.at[c, h, (first[h][0] + 2) % 4], ag1_sem.at[c, h, 2])
        out = jnp.zeros((rows, feat), F32)
        grad = jnp.zeros((rows, feat), F32)
        for b in range(4):
            cols = slice(b * col, (b + 1) * col)
            act, dgate, dup = (
                full[c, b // 2, :, :, b % 2, a].reshape(rows, col) for a in range(3)
            )
            out += dot(act, wd_ref[cols, :], ((1,), (0,)))
            grad += dot(dgate, wg_ref[:, cols], ((1,), (1,)))
            grad += dot(dup, wu_ref[:, cols], ((1,), (1,)))
        ret[c, :, 0:cap, :] = out.astype(BF16).reshape(blocks, cap, feat)
        ret[c, :, cap : 2 * cap, :] = grad.astype(BF16).reshape(blocks, cap, feat)

        def go(k):
            there = ((z + chunks * (k // 2) + c) % zs) * 2 + (core if k % 2 == 0 else 1 - core)
            pltpu.make_async_remote_copy(
                src_ref=ret.at[c, k],
                dst_ref=back.at[me],
                send_sem=back_send,
                recv_sem=back_recv,
                device_id=(dp, there),
                device_id_type=MESH,
            ).start()

        @pl.when(c == 0)
        def _():
            pltpu.make_async_copy(ret.at[c, 0], back.at[me], back_recv).start()

        @pl.when(c > 0)
        def _():
            go(0)

        for k in range(1, blocks):
            go(k)

        x = recv[c, :, 0:cap, :].reshape(rows, feat)
        g = recv[c, :, cap : 2 * cap, :].reshape(rows, feat)
        for b in range(4):
            cols = slice(b * col, (b + 1) * col)
            act, dgate, dup = (
                full[c, b // 2, :, :, b % 2, a].reshape(rows, col) for a in range(3)
            )
            acc_g[:, cols] += dot(x, dgate, ((0,), (0,)))
            acc_u[:, cols] += dot(x, dup, ((0,), (0,)))
            acc_d[cols, :] += dot(act, g, ((0,), (0,)))

    stages = (
        stage_partials,
        stage_relay1,
        stage_second,
        stage_relay2,
        stage_pointwise,
        stage_forward2,
        stage_first,
        stage_forward1,
        stage_outputs,
    )

    def step(u, carry):
        for r in range(LAG):
            for s in reversed(range(r, len(stages), LAG)):
                c = u - s // LAG

                @pl.when((c >= 0) & (c < chunks))
                def _(s=s, c=c):
                    stages[s](c)

        return carry

    lax.fori_loop(0, (len(stages) - 1) // LAG + chunks, step, 0)

    ggate_ref[...] = acc_g[...].astype(BF16)
    gup_ref[...] = acc_u[...].astype(BF16)
    gdown_ref[...] = acc_d[...].astype(BF16)

    wait_bytes(back, back_recv)
    sel = pick[...]
    token_out = dot(sel, back[:, 0:cap, :].reshape(slots, feat), ((1,), (0,)))
    mixed_ref[...] = (weight * token_out).astype(BF16)
    gtok_ref[...] = dot(
        sel, back[:, cap : 2 * cap, :].reshape(slots, feat), ((1,), (0,))
    ).astype(BF16)

    wait_bytes(send.at[0 : experts - 1], disp_send)
    wait_bytes(back.at[0 : experts - 1], back_send)
    for c in range(chunks):
        wait_bytes(part.at[c, 0:3], xy_send.at[c, 0])
        wait_bytes(red.at[c, 0:3], xy_send.at[c, 1])
        wait_bytes(full.at[c, :, 0, 0:3], xy_send.at[c, 2])
        wait_bytes(full.at[c, :, 0:3], xy_send.at[c, 3])


def body(tokens, grad_out, expert_ids, gates, w_gate, w_up, w_down):
    experts = lax.axis_size("expert")
    toks, feat = tokens.shape
    hid = w_gate.shape[-1]
    cap = toks // 16
    zs = experts // 2
    chunks = 4 if zs % 4 == 0 else zs
    rows = experts * cap // chunks
    q1, q2, col = rows // 4, rows // 16, hid // 4
    dma = pltpu.SemaphoreType.DMA
    results = pl.pallas_call(
        functools.partial(kernel, experts, cap, chunks),
        out_shape=(
            jax.ShapeDtypeStruct((toks, feat), BF16),
            jax.ShapeDtypeStruct((toks, feat), BF16),
            jax.ShapeDtypeStruct((feat, hid), BF16),
            jax.ShapeDtypeStruct((feat, hid), BF16),
            jax.ShapeDtypeStruct((hid, feat), BF16),
        ),
        in_specs=[pl.BlockSpec(memory_space=pltpu.VMEM)] * 7,
        out_specs=(pl.BlockSpec(memory_space=pltpu.VMEM),) * 5,
        scratch_shapes=[
            pltpu.VMEM((experts, 2 * cap, feat), BF16),
            pltpu.VMEM((chunks, experts // chunks, 2 * cap, feat), BF16),
            pltpu.VMEM((chunks, 4, 4, 3, q1, col), BF16),
            pltpu.VMEM((chunks, 2, 2, 3, q1, col), BF16),
            pltpu.VMEM((chunks, 2, 4, 3, q1, col), BF16),
            pltpu.VMEM((chunks, 4, 4, 3, q2, col), BF16),
            pltpu.VMEM((chunks, 2, 2, 3, q2, col), BF16),
            pltpu.VMEM((chunks, 2, 4, 3, q2, col), BF16),
            pltpu.VMEM((chunks, 2, 4, 4, 2, 3, q2, col), BF16),
            pltpu.VMEM((chunks, experts // chunks, 2 * cap, feat), BF16),
            pltpu.VMEM((experts, 2 * cap, feat), BF16),
            pltpu.VMEM((toks, experts * cap), BF16),
            pltpu.VMEM((feat, hid), F32),
            pltpu.VMEM((feat, hid), F32),
            pltpu.VMEM((hid, feat), F32),
            dma,
            dma((chunks,)),
            dma,
            dma,
            dma((chunks, 4)),
            dma((chunks, 2, 2)),
            dma((chunks, 2)),
            dma((chunks, 2, 2)),
            dma((chunks, 2)),
            dma((chunks, 2, 3)),
            dma((chunks, 2, 3)),
        ],
        compiler_params=pltpu.CompilerParams(
            collective_id=0, has_side_effects=True, vmem_limit_bytes=60 * 1024 * 1024
        ),
    )(tokens, grad_out, expert_ids, gates, w_gate[0], w_up[0], w_down[0])
    mixed, grad_tokens, grad_gate, grad_up, grad_down = results
    return (mixed, grad_tokens, grad_gate[None], grad_up[None], grad_down[None])


def solution(mesh):
    placed = (
        P("expert", "dp"),
        P("expert", "dp"),
        P("expert", None),
        P("expert", None),
        P("expert", "dp", None),
        P("expert", "dp", None),
        P("expert", None, "dp"),
    )
    return jax.shard_map(
        body,
        mesh=mesh,
        in_specs=placed,
        out_specs=(
            P("expert", "dp"),
            P("expert", "dp"),
            P("expert", "dp", None),
            P("expert", "dp", None),
            P("expert", None, "dp"),
        ),
        check_vma=False,
    )
```

```python
import functools

import jax
import jax.numpy as jnp
from jax import lax
from jax.experimental import pallas as pl
from jax.experimental.pallas import tpu as pltpu
from jax.sharding import PartitionSpec as P

MESH = pl.DeviceIdType.MESH
BF16 = jnp.bfloat16
F32 = jnp.float32
RING = 4
STARTS = (0, 1, 4, 5, 7, 8, 11, 12)
LANES = 128


def dot(left, right, dims):
    return lax.dot_general(left, right, (dims, ((), ())), preferred_element_type=F32)


def z_wait(ref, sem):
    pltpu.make_async_copy(ref, ref, sem).wait()


def xy_wait(ref, sem):
    pltpu.make_async_copy(ref, ref, sem).wait()


def z_send(src, dst, send_sem, recv_sem, device):
    pltpu.make_async_remote_copy(src, dst, send_sem, recv_sem, device, MESH).start()


def xy_send_to(src, dst, send_sem, recv_sem, device):
    pltpu.make_async_remote_copy(src, dst, send_sem, recv_sem, device, MESH).start()


def kernel(
    experts,
    cap,
    chunks,
    tok_ref,
    gout_ref,
    ids_ref,
    gates_ref,
    wg_ref,
    wu_ref,
    wd_ref,
    mixed_ref,
    gtok_ref,
    ggate_ref,
    gup_ref,
    gdown_ref,
    send,
    recv,
    part,
    ra1,
    rb1,
    red,
    ra2,
    rb2,
    full,
    ret,
    back,
    place,
    comb,
    wgp,
    wup,
    wdp,
    xs,
    gs,
    acc_g,
    acc_u,
    acc_d,
    disp_send,
    disp_recv,
    back_send,
    back_recv,
    xy_send,
    ra1_sem,
    rb1_sem,
    ra2_sem,
    rb2_sem,
    ag2_sem,
    ag1_sem,
):
    dp = lax.axis_index("dp")
    me = lax.axis_index("expert")
    px, py = dp // RING, dp % RING
    zs = experts // 2
    z, core = me // 2, me % 2
    per = zs // chunks
    blocks = 2 * per
    rows = blocks * cap
    feat, toks = tok_ref.shape
    slots = experts * cap
    col = part.shape[-1]
    q2 = red.shape[-2]

    def peer(dz, dc):
        return ((z + dz) % zs) * 2 + (core if dc == 0 else 1 - core)

    def x_peer(step):
        return ((px + step) % RING) * RING + py

    def y_peer(step):
        return px * RING + (py + step) % RING

    def distance(c, j):
        base = per * c
        if chunks == len(STARTS):
            late = c // (chunks // 2)
            base = 2 * per * ((1 - late) * c + late * (chunks - 1 - c)) + late * per
        k = base + j
        far, odd = (k + 1) // 2, k % 2
        return (odd * far + (1 - odd) * (zs - far)) % zs

    barrier = pltpu.get_barrier_semaphore()
    for dz in range(zs):
        for dc in range(2):
            if dz or dc:
                pl.semaphore_signal(
                    barrier, inc=1, device_id=(dp, peer(dz, dc)), device_id_type=MESH
                )
    for near in (x_peer(1), x_peer(RING - 1), y_peer(1), y_peer(RING - 1)):
        pl.semaphore_signal(barrier, inc=1, device_id=(near, me), device_id_type=MESH)

    ids = ids_ref[...]
    inside = ids < experts
    chosen = jnp.sum(jnp.where(inside, ids, 0).astype(F32), axis=0, keepdims=True)
    routed = jnp.sum(jnp.where(inside, 1.0, 0.0), axis=0, keepdims=True)
    weight = jnp.sum(jnp.where(inside, gates_ref[...], 0.0), axis=0, keepdims=True)
    row_e = lax.broadcasted_iota(jnp.int32, (experts, toks), 0).astype(F32)
    one_hot = jnp.where((row_e == chosen) & (routed > 0.0), 1.0, 0.0)
    earlier = jnp.where(
        lax.broadcasted_iota(jnp.int32, (toks, toks), 0)
        < lax.broadcasted_iota(jnp.int32, (toks, toks), 1),
        1.0,
        0.0,
    ).astype(BF16)
    counts = dot(one_hot.astype(BF16), earlier, ((1,), (0,)))
    position = jnp.sum(counts * one_hot, axis=0, keepdims=True)
    slot = jnp.where(routed > 0.0, chosen * cap + position, 2.0 * slots)
    row_s = lax.broadcasted_iota(jnp.int32, (slots, toks), 0).astype(F32)
    place[...] = jnp.where(row_s == slot, 1.0, 0.0).astype(BF16)
    scaled = (weight * gout_ref[...].astype(F32)).astype(BF16)
    wide = feat - LANES
    cut = 2 * LANES - wide
    comb[0:LANES, :] = tok_ref[0:LANES, :]
    comb[LANES : 2 * LANES, :] = scaled[0:LANES, :]
    comb[2 * LANES : 2 * LANES + wide, :] = tok_ref[LANES:feat, :]
    comb[2 * LANES + wide : 3 * LANES, :] = scaled[LANES:cut, :]
    comb[3 * LANES : 3 * LANES + feat - cut, :] = scaled[cut:feat, :]
    comb[3 * LANES + feat - cut : 4 * LANES, :] = scaled[cut:feat, :]
    laid = dot(place[...], comb[...], ((1,), (1,)))
    for i in range(3):
        send[:, i * cap : (i + 1) * cap, :] = (
            laid[:, i * LANES : (i + 1) * LANES].astype(BF16).reshape(experts, cap, LANES)
        )
    last = laid[:, 3 * LANES : 4 * LANES].reshape(experts, cap, LANES)
    half = cap // 2
    lane = lax.broadcasted_iota(jnp.int32, (1, 1, LANES), 2)
    send[:, 3 * cap : 3 * cap + half, :] = jnp.where(
        lane < LANES // 2, last[:, 0:half, :], last[:, half:cap, :]
    ).astype(BF16)

    pl.semaphore_wait(barrier, 2 * zs - 1 + 4)

    for c in range(chunks):
        for j in range(per):
            for dc in range(2):
                dz = distance(c, j)
                target = recv.at[c, 2 * j + dc]
                if dz == 0 and dc == 0:
                    pltpu.make_async_copy(send.at[me], target, disp_recv.at[c]).start()
                else:
                    there = peer(zs - dz, dc)
                    z_send(send.at[there], target, disp_send, disp_recv.at[c], (dp, there))

    none = jnp.zeros((2 * LANES - feat, wg_ref.shape[1]), BF16)
    for padded, ref in ((wgp, wg_ref), (wup, wu_ref)):
        padded[0:feat, :] = ref[...]
        padded[feat : 2 * LANES, :] = none
    wdp[0:LANES, :] = wd_ref[0:LANES, :]
    wdp[LANES : LANES + feat - cut, :] = wd_ref[cut:feat, :]
    wdp[LANES + feat - cut : LANES + wide, :] = none
    wdp[LANES + wide : 2 * LANES, :] = wd_ref[LANES:cut, :]

    def unpack(rows3, count):
        first_x = rows3[:, 0:cap, :]
        first_g = rows3[:, cap : 2 * cap, :]
        both = rows3[:, 2 * cap : 3 * cap, :]
        pair = rows3[:, 3 * cap : 3 * cap + half, :].astype(F32)
        other = pltpu.roll(pair.reshape(count * half, LANES), LANES // 2, 1)
        pair = jnp.concatenate([pair, other.reshape(count, half, LANES)], axis=1)
        rest = jnp.where(
            lane < LANES // 2, pair, jnp.where(lane >= wide, both.astype(F32), 0.0)
        ).astype(BF16)
        n = count * cap
        return (
            (first_x.reshape(n, LANES), both.reshape(n, LANES)),
            (first_g.reshape(n, LANES), rest.reshape(n, LANES)),
        )

    acc_g[...] = jnp.zeros_like(acc_g)
    acc_u[...] = jnp.zeros_like(acc_u)
    acc_d[...] = jnp.zeros_like(acc_d)

    def hop(src, dst, send_sem, recv_sem, near):
        xy_send_to(src, dst, send_sem, recv_sem, (near, me))

    first = ((px, x_peer(1), x_peer(RING - 1)), (py, y_peer(1), y_peer(RING - 1)))
    second = (first[1], first[0])

    def rs_start(src, ra, rb, c, h, ring, ssem, ra_sem, rb_sem):
        p, right, left = ring
        lo, hi = 2 * h, 2 * h + 1
        hop(src.at[c, lo, (p + 2) % 4], ra.at[c, h, 0], ssem, ra_sem.at[c, h, 0], right)
        hop(src.at[c, hi, (p + 2) % 4], ra.at[c, h, 1], ssem, ra_sem.at[c, h, 1], left)
        hop(src.at[c, hi, (p + 1) % 4], rb.at[c, h, 0], ssem, rb_sem.at[c, h], right)
        hop(src.at[c, lo, (p + 3) % 4], rb.at[c, h, 1], ssem, rb_sem.at[c, h], left)

    def rs_relay(src, ra, rb, c, h, ring, ssem, ra_sem, rb_sem):
        p, right, left = ring
        for side, b, t, near in ((0, 2 * h, (p + 1) % 4, right), (1, 2 * h + 1, (p + 3) % 4, left)):
            xy_wait(ra.at[c, h, side], ra_sem.at[c, h, side])
            src[c, b, t] = (src[c, b, t].astype(F32) + ra[c, h, side].astype(F32)).astype(BF16)
            hop(src.at[c, b, t], rb.at[c, h, 2 + side], ssem, rb_sem.at[c, h], near)

    def rs_final(src, rb, c, h, ring, rb_sem):
        p = ring[0]
        xy_wait(rb.at[c, h], rb_sem.at[c, h])
        lo = src[c, 2 * h, p].astype(F32) + rb[c, h, 1].astype(F32) + rb[c, h, 2].astype(F32)
        hi = src[c, 2 * h + 1, p].astype(F32) + rb[c, h, 0].astype(F32) + rb[c, h, 3].astype(F32)
        return lo, hi

    def stage_partials(c):
        z_wait(recv.at[c], disp_recv.at[c])
        x_pair, g_pair = unpack(recv[c], blocks)
        for i in range(2):
            xs[c, :, i * LANES : (i + 1) * LANES] = x_pair[i]
            gs[c, :, i * LANES : (i + 1) * LANES] = g_pair[i]
        x = xs[c]
        g = gs[c]
        for h in range(2):
            for b in (2 * h, 2 * h + 1):
                cols = slice(b * col, (b + 1) * col)
                terms = (
                    dot(x, wgp[:, cols], ((1,), (0,))),
                    dot(x, wup[:, cols], ((1,), (0,))),
                    dot(g, wdp[:, cols], ((1,), (0,))),
                )
                for a in range(3):
                    part[c, b, :, a] = terms[a].astype(BF16).reshape(4, rows // 4, col)
            rs_start(part, ra1, rb1, c, h, first[h], xy_send.at[c, 0], ra1_sem, rb1_sem)

    def stage_relay1(c):
        for h in range(2):
            rs_relay(part, ra1, rb1, c, h, first[h], xy_send.at[c, 0], ra1_sem, rb1_sem)

    def stage_second(c):
        for h in range(2):
            sums = rs_final(part, rb1, c, h, first[h], rb1_sem)
            for side in range(2):
                for a in range(3):
                    red[c, 2 * h + side, :, a] = sums[side][a].astype(BF16).reshape(4, q2, col)
            rs_start(red, ra2, rb2, c, h, second[h], xy_send.at[c, 1], ra2_sem, rb2_sem)

    def stage_relay2(c):
        for h in range(2):
            rs_relay(red, ra2, rb2, c, h, second[h], xy_send.at[c, 1], ra2_sem, rb2_sem)

    def stage_pointwise(c):
        for h in range(2):
            p1 = first[h][0]
            p2, right, left = second[h]
            sums = rs_final(red, rb2, c, h, second[h], rb2_sem)
            for side in range(2):
                gate, up, grad = sums[side][0], sums[side][1], sums[side][2]
                logistic = 1.0 / (1.0 + jnp.exp(-gate))
                swish = gate * logistic
                full[c, h, p1, p2, side, 0] = (swish * up).astype(BF16)
                full[c, h, p1, p2, side, 1] = (
                    grad * up * (logistic * (1.0 + gate * (1.0 - logistic)))
                ).astype(BF16)
                full[c, h, p1, p2, side, 2] = (grad * swish).astype(BF16)
            own = full.at[c, h, p1, p2]
            hop(own, own, xy_send.at[c, 2], ag2_sem.at[c, h, 0], right)
            hop(own, own, xy_send.at[c, 2], ag2_sem.at[c, h, 1], left)

    def stage_forward2(c):
        for h in range(2):
            p1 = first[h][0]
            p2, right, left = second[h]
            for side, t, near in ((0, (p2 + 3) % 4, right), (1, (p2 + 1) % 4, left)):
                xy_wait(full.at[c, h, p1, t], ag2_sem.at[c, h, side])
                piece = full.at[c, h, p1, t, side]
                hop(piece, piece, xy_send.at[c, 2], ag2_sem.at[c, h, 2], near)

    def stage_first(c):
        for h in range(2):
            p1, right, left = first[h]
            p2 = second[h][0]
            xy_wait(full.at[c, h, p1, (p2 + 2) % 4], ag2_sem.at[c, h, 2])
            own = full.at[c, h, p1]
            hop(own, own, xy_send.at[c, 3], ag1_sem.at[c, h, 0], right)
            hop(own, own, xy_send.at[c, 3], ag1_sem.at[c, h, 1], left)

    def stage_forward1(c):
        for h in range(2):
            p1, right, left = first[h]
            for side, t, near in ((0, (p1 + 3) % 4, right), (1, (p1 + 1) % 4, left)):
                xy_wait(full.at[c, h, t], ag1_sem.at[c, h, side])
                piece = full.at[c, h, t, :, side]
                hop(piece, piece, xy_send.at[c, 3], ag1_sem.at[c, h, 2], near)

    def stage_outputs(c):
        for h in range(2):
            xy_wait(full.at[c, h, (first[h][0] + 2) % 4], ag1_sem.at[c, h, 2])
        out = jnp.zeros((rows, 2 * LANES), F32)
        grad = jnp.zeros((rows, 2 * LANES), F32)
        for b in range(4):
            cols = slice(b * col, (b + 1) * col)
            act, dgate, dup = (
                full[c, b // 2, :, :, b % 2, a].reshape(rows, col) for a in range(3)
            )
            out += dot(act, wdp[:, cols], ((1,), (1,)))
            grad += dot(dgate, wgp[:, cols], ((1,), (1,)))
            grad += dot(dup, wup[:, cols], ((1,), (1,)))
        packed = (blocks, cap, LANES)
        rest = out[:, LANES : 2 * LANES].reshape(packed)
        turned = pltpu.roll(rest[:, half:cap, :].reshape(blocks * half, LANES), LANES // 2, 1)
        ret[c, :, 0:cap, :] = grad[:, 0:LANES].astype(BF16).reshape(packed)
        ret[c, :, cap : 2 * cap, :] = out[:, 0:LANES].astype(BF16).reshape(packed)
        ret[c, :, 2 * cap : 3 * cap, :] = jnp.where(
            lane < wide, grad[:, LANES : 2 * LANES].reshape(packed), rest
        ).astype(BF16)
        ret[c, :, 3 * cap : 3 * cap + half, :] = jnp.where(
            lane < LANES // 2, rest[:, 0:half, :], turned.reshape(blocks, half, LANES)
        ).astype(BF16)

        def go(k):
            there = peer(distance(c, k // 2), k % 2)
            z_send(ret.at[c, k], back.at[me], back_send, back_recv, (dp, there))

        @pl.when(c == 0)
        def _():
            pltpu.make_async_copy(ret.at[c, 0], back.at[me], back_recv).start()

        @pl.when(c > 0)
        def _():
            go(0)

        for k in range(1, blocks):
            go(k)

        x = xs[c]
        g = gs[c]
        for b in range(4):
            cols = slice(b * col, (b + 1) * col)
            act, dgate, dup = (
                full[c, b // 2, :, :, b % 2, a].reshape(rows, col) for a in range(3)
            )
            acc_g[:, cols] += dot(x, dgate, ((0,), (0,)))
            acc_u[:, cols] += dot(x, dup, ((0,), (0,)))
            acc_d[:, cols] += dot(g, act, ((0,), (0,)))

    stages = (
        stage_partials,
        stage_relay1,
        stage_second,
        stage_relay2,
        stage_pointwise,
        stage_forward2,
        stage_first,
        stage_forward1,
        stage_outputs,
    )

    starts = STARTS[:chunks]

    def step(t, carry):
        for s in reversed(range(len(stages))):
            since = t - s
            c = sum((since >= begin).astype(jnp.int32) for begin in starts[1:])

            @pl.when(functools.reduce(jnp.logical_or, [since == begin for begin in starts]))
            def _(s=s, c=c):
                stages[s](c)

        return carry

    lax.fori_loop(0, len(stages) + starts[-1], step, 0)

    def restore(ref, value):
        ref[0:LANES, :] = value[0:LANES].astype(BF16)
        ref[LANES:cut, :] = value[LANES + wide : 2 * LANES].astype(BF16)
        ref[cut:feat, :] = value[LANES : LANES + feat - cut].astype(BF16)

    ggate_ref[...] = acc_g[0:feat, :].astype(BF16)
    gup_ref[...] = acc_u[0:feat, :].astype(BF16)
    restore(gdown_ref, acc_d[...])

    z_wait(back, back_recv)
    grad_pair, out_pair = unpack(back[...], experts)
    spots = ((0,), (0,))
    restore(mixed_ref, weight * dot(jnp.concatenate(out_pair, axis=1), place[...], spots))
    gtok_ref[...] = dot(jnp.concatenate(grad_pair, axis=1), place[...], spots)[0:feat].astype(BF16)

    z_wait(send.at[0 : experts - 1], disp_send)
    z_wait(back.at[0 : experts - 1], back_send)
    for c in range(chunks):
        xy_wait(part.at[c, 0:3], xy_send.at[c, 0])
        xy_wait(red.at[c, 0:3], xy_send.at[c, 1])
        xy_wait(full.at[c, :, 0, 0:3], xy_send.at[c, 2])
        xy_wait(full.at[c, :, 0:3], xy_send.at[c, 3])


def body(tokens, grad_out, expert_ids, gates, w_gate, w_up, w_down):
    experts = lax.axis_size("expert")
    toks, feat = tokens.shape
    hid = w_gate.shape[-1]
    cap = toks // 16
    zs = experts // 2
    chunks = min(len(STARTS), zs)
    rows = experts * cap // chunks
    q1, q2, col = rows // 4, rows // 16, hid // 4
    packed = 3 * cap + cap // 2
    dma = pltpu.SemaphoreType.DMA
    results = pl.pallas_call(
        functools.partial(kernel, experts, cap, chunks),
        out_shape=(
            jax.ShapeDtypeStruct((feat, toks), BF16),
            jax.ShapeDtypeStruct((feat, toks), BF16),
            jax.ShapeDtypeStruct((feat, hid), BF16),
            jax.ShapeDtypeStruct((feat, hid), BF16),
            jax.ShapeDtypeStruct((feat, hid), BF16),
        ),
        in_specs=[pl.BlockSpec(memory_space=pltpu.VMEM)] * 7,
        out_specs=(pl.BlockSpec(memory_space=pltpu.VMEM),) * 5,
        scratch_shapes=[
            pltpu.VMEM((experts, packed, LANES), BF16),
            pltpu.VMEM((chunks, experts // chunks, packed, LANES), BF16),
            pltpu.VMEM((chunks, 4, 4, 3, q1, col), BF16),
            pltpu.VMEM((chunks, 2, 2, 3, q1, col), BF16),
            pltpu.VMEM((chunks, 2, 4, 3, q1, col), BF16),
            pltpu.VMEM((chunks, 4, 4, 3, q2, col), BF16),
            pltpu.VMEM((chunks, 2, 2, 3, q2, col), BF16),
            pltpu.VMEM((chunks, 2, 4, 3, q2, col), BF16),
            pltpu.VMEM((chunks, 2, 4, 4, 2, 3, q2, col), BF16),
            pltpu.VMEM((chunks, experts // chunks, packed, LANES), BF16),
            pltpu.VMEM((experts, packed, LANES), BF16),
            pltpu.VMEM((experts * cap, toks), BF16),
            pltpu.VMEM((4 * LANES, toks), BF16),
            pltpu.VMEM((2 * LANES, hid), BF16),
            pltpu.VMEM((2 * LANES, hid), BF16),
            pltpu.VMEM((2 * LANES, hid), BF16),
            pltpu.VMEM((chunks, rows, 2 * LANES), BF16),
            pltpu.VMEM((chunks, rows, 2 * LANES), BF16),
            pltpu.VMEM((2 * LANES, hid), F32),
            pltpu.VMEM((2 * LANES, hid), F32),
            pltpu.VMEM((2 * LANES, hid), F32),
            dma,
            dma((chunks,)),
            dma,
            dma,
            dma((chunks, 4)),
            dma((chunks, 2, 2)),
            dma((chunks, 2)),
            dma((chunks, 2, 2)),
            dma((chunks, 2)),
            dma((chunks, 2, 3)),
            dma((chunks, 2, 3)),
        ],
        compiler_params=pltpu.CompilerParams(
            collective_id=0, has_side_effects=True, vmem_limit_bytes=60 * 1024 * 1024
        ),
    )(tokens.T, grad_out.T, expert_ids.T, gates.T, w_gate[0], w_up[0], w_down[0].T)
    mixed, grad_tokens, grad_gate, grad_up, grad_down = results
    return (mixed.T, grad_tokens.T, grad_gate[None], grad_up[None], grad_down.T[None])


def solution(mesh):
    placed = (
        P("expert", "dp"),
        P("expert", "dp"),
        P("expert", None),
        P("expert", None),
        P("expert", "dp", None),
        P("expert", "dp", None),
        P("expert", None, "dp"),
    )
    return jax.shard_map(
        body,
        mesh=mesh,
        in_specs=placed,
        out_specs=(
            P("expert", "dp"),
            P("expert", "dp"),
            P("expert", "dp", None),
            P("expert", "dp", None),
            P("expert", None, "dp"),
        ),
        check_vma=False,
    )
```

```python
import functools

import jax
import jax.numpy as jnp
from jax import lax
from jax.experimental import pallas as pl
from jax.experimental.pallas import tpu as pltpu
from jax.sharding import PartitionSpec as P

MESH = pl.DeviceIdType.MESH
BF16 = jnp.bfloat16
F32 = jnp.float32
RING = 4
STARTS = (0, 1, 4, 5, 7, 8, 11, 12)
LANES = 128


def dot(left, right, dims):
    return lax.dot_general(left, right, (dims, ((), ())), preferred_element_type=F32)


def z_wait(ref, sem):
    pltpu.make_async_copy(ref, ref, sem).wait()


def xy_wait(ref, sem):
    pltpu.make_async_copy(ref, ref, sem).wait()


def z_send(src, dst, send_sem, recv_sem, device):
    pltpu.make_async_remote_copy(src, dst, send_sem, recv_sem, device, MESH).start()


def xy_send_to(src, dst, send_sem, recv_sem, device):
    pltpu.make_async_remote_copy(src, dst, send_sem, recv_sem, device, MESH).start()


def kernel(
    experts,
    cap,
    chunks,
    tok_ref,
    gout_ref,
    ids_ref,
    gates_ref,
    wg_ref,
    wu_ref,
    wd_ref,
    mixed_ref,
    gtok_ref,
    ggate_ref,
    gup_ref,
    gdown_ref,
    send,
    recv,
    part,
    ra1,
    rb1,
    red,
    ra2,
    rb2,
    full,
    ret,
    back,
    place,
    comb,
    wgp,
    wup,
    wdp,
    xs,
    gs,
    out_m,
    out_t,
    out_g,
    out_u,
    out_d,
    in_sem,
    out_sem,
    disp_send,
    disp_recv,
    back_send,
    back_recv,
    xy_send,
    ra1_sem,
    rb1_sem,
    ra2_sem,
    rb2_sem,
    ag2_sem,
    ag1_sem,
):
    dp = lax.axis_index("dp")
    me = lax.axis_index("expert")
    px, py = dp // RING, dp % RING
    zs = experts // 2
    z, core = me // 2, me % 2
    per = zs // chunks
    blocks = 2 * per
    rows = blocks * cap
    feat, toks = tok_ref.shape
    slots = experts * cap
    col = part.shape[-1]
    q2 = red.shape[-2]

    def peer(dz, dc):
        return ((z + dz) % zs) * 2 + (core if dc == 0 else 1 - core)

    def x_peer(step):
        return ((px + step) % RING) * RING + py

    def y_peer(step):
        return px * RING + (py + step) % RING

    def distance(c, j):
        base = per * c
        if chunks == len(STARTS):
            late = c // (chunks // 2)
            base = 2 * per * ((1 - late) * c + late * (chunks - 1 - c)) + late * per
        k = base + j
        far, odd = (k + 1) // 2, k % 2
        return (odd * far + (1 - odd) * (zs - far)) % zs

    barrier = pltpu.get_barrier_semaphore()
    for dz in range(zs):
        for dc in range(2):
            if dz or dc:
                pl.semaphore_signal(
                    barrier, inc=1, device_id=(dp, peer(dz, dc)), device_id_type=MESH
                )
    for near in (x_peer(1), x_peer(RING - 1), y_peer(1), y_peer(RING - 1)):
        pl.semaphore_signal(barrier, inc=1, device_id=(near, me), device_id_type=MESH)

    wide = feat - LANES
    cut = 2 * LANES - wide
    pieces = (
        (wg_ref, wgp.at[0:feat]),
        (wu_ref, wup.at[0:feat]),
        (wd_ref.at[0:LANES], wdp.at[0:LANES]),
        (wd_ref.at[cut:feat], wdp.at[LANES : LANES + feat - cut]),
        (wd_ref.at[LANES:cut], wdp.at[LANES + wide : 2 * LANES]),
    )
    loads = [pltpu.make_async_copy(pair[0], pair[1], in_sem.at[i]) for i, pair in enumerate(pieces)]
    for load in loads:
        load.start()
    wgp[feat : 2 * LANES, :] = jnp.zeros((2 * LANES - feat, wgp.shape[1]), BF16)
    wup[feat : 2 * LANES, :] = jnp.zeros((2 * LANES - feat, wgp.shape[1]), BF16)
    wdp[LANES + feat - cut : LANES + wide, :] = jnp.zeros((wide + cut - feat, wgp.shape[1]), BF16)

    ids = ids_ref[...]
    inside = ids < experts
    chosen = jnp.sum(jnp.where(inside, ids, 0).astype(F32), axis=0, keepdims=True)
    routed = jnp.sum(jnp.where(inside, 1.0, 0.0), axis=0, keepdims=True)
    weight = jnp.sum(jnp.where(inside, gates_ref[...], 0.0), axis=0, keepdims=True)
    row_e = lax.broadcasted_iota(jnp.int32, (experts, toks), 0).astype(F32)
    one_hot = jnp.where((row_e == chosen) & (routed > 0.0), 1.0, 0.0)
    earlier = jnp.where(
        lax.broadcasted_iota(jnp.int32, (toks, toks), 0)
        < lax.broadcasted_iota(jnp.int32, (toks, toks), 1),
        1.0,
        0.0,
    ).astype(BF16)
    counts = dot(one_hot.astype(BF16), earlier, ((1,), (0,)))
    position = jnp.sum(counts * one_hot, axis=0, keepdims=True)
    slot = jnp.where(routed > 0.0, chosen * cap + position, 2.0 * slots)
    row_s = lax.broadcasted_iota(jnp.int32, (slots, toks), 0).astype(F32)
    place[...] = jnp.where(row_s == slot, 1.0, 0.0).astype(BF16)
    scaled = (weight * gout_ref[...].astype(F32)).astype(BF16)
    comb[0:LANES, :] = tok_ref[0:LANES, :]
    comb[LANES : 2 * LANES, :] = scaled[0:LANES, :]
    comb[2 * LANES : 2 * LANES + wide, :] = tok_ref[LANES:feat, :]
    comb[2 * LANES + wide : 3 * LANES, :] = scaled[LANES:cut, :]
    comb[3 * LANES : 3 * LANES + feat - cut, :] = scaled[cut:feat, :]
    comb[3 * LANES + feat - cut : 4 * LANES, :] = scaled[cut:feat, :]
    laid = dot(place[...], comb[...], ((1,), (1,)))
    for i in range(3):
        send[:, i * cap : (i + 1) * cap, :] = (
            laid[:, i * LANES : (i + 1) * LANES].astype(BF16).reshape(experts, cap, LANES)
        )
    last = laid[:, 3 * LANES : 4 * LANES].reshape(experts, cap, LANES)
    half = cap // 2
    lane = lax.broadcasted_iota(jnp.int32, (1, 1, LANES), 2)
    send[:, 3 * cap : 3 * cap + half, :] = jnp.where(
        lane < LANES // 2, last[:, 0:half, :], last[:, half:cap, :]
    ).astype(BF16)

    pl.semaphore_wait(barrier, 2 * zs - 1 + 4)

    for c in range(chunks):
        for j in range(per):
            for dc in range(2):
                dz = distance(c, j)
                target = recv.at[c, 2 * j + dc]
                if dz == 0 and dc == 0:
                    pltpu.make_async_copy(send.at[me], target, disp_recv.at[c]).start()
                else:
                    there = peer(zs - dz, dc)
                    z_send(send.at[there], target, disp_send, disp_recv.at[c], (dp, there))

    def unpack(rows3, count):
        first_x = rows3[:, 0:cap, :]
        first_g = rows3[:, cap : 2 * cap, :]
        both = rows3[:, 2 * cap : 3 * cap, :]
        pair = rows3[:, 3 * cap : 3 * cap + half, :].astype(F32)
        other = pltpu.roll(pair.reshape(count * half, LANES), LANES // 2, 1)
        pair = jnp.concatenate([pair, other.reshape(count, half, LANES)], axis=1)
        rest = jnp.where(
            lane < LANES // 2, pair, jnp.where(lane >= wide, both.astype(F32), 0.0)
        ).astype(BF16)
        n = count * cap
        return (
            (first_x.reshape(n, LANES), both.reshape(n, LANES)),
            (first_g.reshape(n, LANES), rest.reshape(n, LANES)),
        )

    for load in loads:
        load.wait()

    def hop(src, dst, send_sem, recv_sem, near):
        xy_send_to(src, dst, send_sem, recv_sem, (near, me))

    first = ((px, x_peer(1), x_peer(RING - 1)), (py, y_peer(1), y_peer(RING - 1)))
    second = (first[1], first[0])

    def rs_start(src, ra, rb, c, h, ring, ssem, ra_sem, rb_sem):
        p, right, left = ring
        lo, hi = 2 * h, 2 * h + 1
        hop(src.at[c, lo, (p + 2) % 4], ra.at[c, h, 0], ssem, ra_sem.at[c, h, 0], right)
        hop(src.at[c, hi, (p + 2) % 4], ra.at[c, h, 1], ssem, ra_sem.at[c, h, 1], left)
        hop(src.at[c, hi, (p + 1) % 4], rb.at[c, h, 0], ssem, rb_sem.at[c, h], right)
        hop(src.at[c, lo, (p + 3) % 4], rb.at[c, h, 1], ssem, rb_sem.at[c, h], left)

    def rs_relay(src, ra, rb, c, h, ring, ssem, ra_sem, rb_sem):
        p, right, left = ring
        for side, b, t, near in ((0, 2 * h, (p + 1) % 4, right), (1, 2 * h + 1, (p + 3) % 4, left)):
            xy_wait(ra.at[c, h, side], ra_sem.at[c, h, side])
            src[c, b, t] = (src[c, b, t].astype(F32) + ra[c, h, side].astype(F32)).astype(BF16)
            hop(src.at[c, b, t], rb.at[c, h, 2 + side], ssem, rb_sem.at[c, h], near)

    def rs_final(src, rb, c, h, ring, rb_sem):
        p = ring[0]
        xy_wait(rb.at[c, h], rb_sem.at[c, h])
        lo = src[c, 2 * h, p].astype(F32) + rb[c, h, 1].astype(F32) + rb[c, h, 2].astype(F32)
        hi = src[c, 2 * h + 1, p].astype(F32) + rb[c, h, 0].astype(F32) + rb[c, h, 3].astype(F32)
        return lo, hi

    def stage_partials(c):
        z_wait(recv.at[c], disp_recv.at[c])
        x_pair, g_pair = unpack(recv[c], blocks)
        for i in range(2):
            xs[c, :, i * LANES : (i + 1) * LANES] = x_pair[i]
            gs[c, :, i * LANES : (i + 1) * LANES] = g_pair[i]
        x = xs[c]
        g = gs[c]
        for h in range(2):
            for b in (2 * h, 2 * h + 1):
                cols = slice(b * col, (b + 1) * col)
                terms = (
                    dot(x, wgp[:, cols], ((1,), (0,))),
                    dot(x, wup[:, cols], ((1,), (0,))),
                    dot(g, wdp[:, cols], ((1,), (0,))),
                )
                for a in range(3):
                    part[c, b, :, a] = terms[a].astype(BF16).reshape(4, rows // 4, col)
            rs_start(part, ra1, rb1, c, h, first[h], xy_send.at[c, 0], ra1_sem, rb1_sem)

    def stage_relay1(c):
        for h in range(2):
            rs_relay(part, ra1, rb1, c, h, first[h], xy_send.at[c, 0], ra1_sem, rb1_sem)

    def stage_second(c):
        for h in range(2):
            sums = rs_final(part, rb1, c, h, first[h], rb1_sem)
            for side in range(2):
                for a in range(3):
                    red[c, 2 * h + side, :, a] = sums[side][a].astype(BF16).reshape(4, q2, col)
            rs_start(red, ra2, rb2, c, h, second[h], xy_send.at[c, 1], ra2_sem, rb2_sem)

    def stage_relay2(c):
        for h in range(2):
            rs_relay(red, ra2, rb2, c, h, second[h], xy_send.at[c, 1], ra2_sem, rb2_sem)

    def stage_pointwise(c):
        for h in range(2):
            p1 = first[h][0]
            p2, right, left = second[h]
            sums = rs_final(red, rb2, c, h, second[h], rb2_sem)
            for side in range(2):
                gate, up, grad = sums[side][0], sums[side][1], sums[side][2]
                logistic = 1.0 / (1.0 + jnp.exp(-gate))
                swish = gate * logistic
                full[c, h, p1, p2, side, 0] = (swish * up).astype(BF16)
                full[c, h, p1, p2, side, 1] = (
                    grad * up * (logistic * (1.0 + gate * (1.0 - logistic)))
                ).astype(BF16)
                full[c, h, p1, p2, side, 2] = (grad * swish).astype(BF16)
            own = full.at[c, h, p1, p2]
            hop(own, own, xy_send.at[c, 2], ag2_sem.at[c, h, 0], right)
            hop(own, own, xy_send.at[c, 2], ag2_sem.at[c, h, 1], left)

    def stage_forward2(c):
        for h in range(2):
            p1 = first[h][0]
            p2, right, left = second[h]
            for side, t, near in ((0, (p2 + 3) % 4, right), (1, (p2 + 1) % 4, left)):
                xy_wait(full.at[c, h, p1, t], ag2_sem.at[c, h, side])
                piece = full.at[c, h, p1, t, side]
                hop(piece, piece, xy_send.at[c, 2], ag2_sem.at[c, h, 2], near)

    def stage_first(c):
        for h in range(2):
            p1, right, left = first[h]
            p2 = second[h][0]
            xy_wait(full.at[c, h, p1, (p2 + 2) % 4], ag2_sem.at[c, h, 2])
            own = full.at[c, h, p1]
            hop(own, own, xy_send.at[c, 3], ag1_sem.at[c, h, 0], right)
            hop(own, own, xy_send.at[c, 3], ag1_sem.at[c, h, 1], left)

    def stage_forward1(c):
        for h in range(2):
            p1, right, left = first[h]
            for side, t, near in ((0, (p1 + 3) % 4, right), (1, (p1 + 1) % 4, left)):
                xy_wait(full.at[c, h, t], ag1_sem.at[c, h, side])
                piece = full.at[c, h, t, :, side]
                hop(piece, piece, xy_send.at[c, 3], ag1_sem.at[c, h, 2], near)

    def stage_outputs(c):
        for h in range(2):
            xy_wait(full.at[c, h, (first[h][0] + 2) % 4], ag1_sem.at[c, h, 2])
        out = jnp.zeros((rows, 2 * LANES), F32)
        grad = jnp.zeros((rows, 2 * LANES), F32)
        for b in range(4):
            cols = slice(b * col, (b + 1) * col)
            act, dgate, dup = (
                full[c, b // 2, :, :, b % 2, a].reshape(rows, col) for a in range(3)
            )
            out += dot(act, wdp[:, cols], ((1,), (1,)))
            grad += dot(dgate, wgp[:, cols], ((1,), (1,)))
            grad += dot(dup, wup[:, cols], ((1,), (1,)))
        packed = (blocks, cap, LANES)
        rest = out[:, LANES : 2 * LANES].reshape(packed)
        turned = pltpu.roll(rest[:, half:cap, :].reshape(blocks * half, LANES), LANES // 2, 1)
        ret[c, :, 0:cap, :] = grad[:, 0:LANES].astype(BF16).reshape(packed)
        ret[c, :, cap : 2 * cap, :] = out[:, 0:LANES].astype(BF16).reshape(packed)
        ret[c, :, 2 * cap : 3 * cap, :] = jnp.where(
            lane < wide, grad[:, LANES : 2 * LANES].reshape(packed), rest
        ).astype(BF16)
        ret[c, :, 3 * cap : 3 * cap + half, :] = jnp.where(
            lane < LANES // 2, rest[:, 0:half, :], turned.reshape(blocks, half, LANES)
        ).astype(BF16)

        def go(k):
            there = peer(distance(c, k // 2), k % 2)
            z_send(ret.at[c, k], back.at[me], back_send, back_recv, (dp, there))

        @pl.when(c == 0)
        def _():
            pltpu.make_async_copy(ret.at[c, 0], back.at[me], back_recv).start()

        @pl.when(c > 0)
        def _():
            go(0)

        for k in range(1, blocks):
            go(k)

    stages = (
        stage_partials,
        stage_relay1,
        stage_second,
        stage_relay2,
        stage_pointwise,
        stage_forward2,
        stage_first,
        stage_forward1,
        stage_outputs,
    )

    starts = STARTS[:chunks]

    def step(t, carry):
        for s in reversed(range(len(stages))):
            since = t - s
            c = sum((since >= begin).astype(jnp.int32) for begin in starts[1:])

            @pl.when(functools.reduce(jnp.logical_or, [since == begin for begin in starts]))
            def _(s=s, c=c):
                stages[s](c)

        return carry

    lax.fori_loop(0, len(stages) + starts[-1], step, 0)

    def restore(ref, value):
        ref[0:LANES, :] = value[0:LANES].astype(BF16)
        ref[LANES:cut, :] = value[LANES + wide : 2 * LANES].astype(BF16)
        ref[cut:feat, :] = value[LANES : LANES + feat - cut].astype(BF16)

    x_t = xs[...].reshape(slots, 2 * LANES).T
    g_t = gs[...].reshape(slots, 2 * LANES).T
    for b in range(4):
        cols = slice(b * col, (b + 1) * col)
        act, dgate, dup = (
            full[:, b // 2, :, :, b % 2, a].reshape(slots, col) for a in range(3)
        )
        out_g[:, cols] = dot(x_t, dgate, ((1,), (0,)))[0:feat].astype(BF16)
        out_u[:, cols] = dot(x_t, dup, ((1,), (0,)))[0:feat].astype(BF16)
        restore(out_d.at[:, cols], dot(g_t, act, ((1,), (0,))))

    def leave(i, src, dst):
        out = pltpu.make_async_copy(src, dst, out_sem.at[i])
        out.start()
        return out

    outs = [leave(0, out_g, ggate_ref), leave(1, out_u, gup_ref), leave(2, out_d, gdown_ref)]

    z_wait(back, back_recv)
    grad_pair, out_pair = unpack(back[...], experts)
    spots = ((0,), (0,))
    restore(out_m, weight * dot(jnp.concatenate(out_pair, axis=1), place[...], spots))
    outs.append(leave(3, out_m, mixed_ref))
    out_t[...] = dot(jnp.concatenate(grad_pair, axis=1), place[...], spots)[0:feat].astype(BF16)
    outs.append(leave(4, out_t, gtok_ref))

    z_wait(send.at[0 : experts - 1], disp_send)
    z_wait(back.at[0 : experts - 1], back_send)
    for c in range(chunks):
        xy_wait(part.at[c, 0:3], xy_send.at[c, 0])
        xy_wait(red.at[c, 0:3], xy_send.at[c, 1])
        xy_wait(full.at[c, :, 0, 0:3], xy_send.at[c, 2])
        xy_wait(full.at[c, :, 0:3], xy_send.at[c, 3])
    for out in outs:
        out.wait()


def deliver(*refs):
    sources, targets, held = refs[0:5], refs[5:10], refs[10:15]
    in_sem, out_sem = refs[15:17]
    ins = [pltpu.make_async_copy(sources[i], held[i], in_sem.at[i]) for i in range(5)]
    outs = [pltpu.make_async_copy(held[i], targets[i], out_sem.at[i]) for i in range(5)]
    for copy in ins:
        copy.start()
    for i in range(5):
        ins[i].wait()
        outs[i].start()
    for copy in outs:
        copy.wait()


def body(tokens, grad_out, expert_ids, gates, w_gate, w_up, w_down):
    experts = lax.axis_size("expert")
    toks, feat = tokens.shape
    hid = w_gate.shape[-1]
    cap = toks // 16
    zs = experts // 2
    chunks = min(len(STARTS), zs)
    rows = experts * cap // chunks
    q1, q2, col = rows // 4, rows // 16, hid // 4
    packed = 3 * cap + cap // 2
    dma = pltpu.SemaphoreType.DMA
    shapes = (
        jax.ShapeDtypeStruct((feat, toks), BF16),
        jax.ShapeDtypeStruct((feat, toks), BF16),
        jax.ShapeDtypeStruct((feat, hid), BF16),
        jax.ShapeDtypeStruct((feat, hid), BF16),
        jax.ShapeDtypeStruct((feat, hid), BF16),
    )
    anywhere = pl.BlockSpec(memory_space=pl.ANY)
    results = pl.pallas_call(
        functools.partial(kernel, experts, cap, chunks),
        out_shape=shapes,
        in_specs=[pl.BlockSpec(memory_space=pltpu.VMEM)] * 4 + [anywhere] * 3,
        out_specs=(anywhere,) * 5,
        scratch_shapes=[
            pltpu.VMEM((experts, packed, LANES), BF16),
            pltpu.VMEM((chunks, experts // chunks, packed, LANES), BF16),
            pltpu.VMEM((chunks, 4, 4, 3, q1, col), BF16),
            pltpu.VMEM((chunks, 2, 2, 3, q1, col), BF16),
            pltpu.VMEM((chunks, 2, 4, 3, q1, col), BF16),
            pltpu.VMEM((chunks, 4, 4, 3, q2, col), BF16),
            pltpu.VMEM((chunks, 2, 2, 3, q2, col), BF16),
            pltpu.VMEM((chunks, 2, 4, 3, q2, col), BF16),
            pltpu.VMEM((chunks, 2, 4, 4, 2, 3, q2, col), BF16),
            pltpu.VMEM((chunks, experts // chunks, packed, LANES), BF16),
            pltpu.VMEM((experts, packed, LANES), BF16),
            pltpu.VMEM((experts * cap, toks), BF16),
            pltpu.VMEM((4 * LANES, toks), BF16),
            pltpu.VMEM((2 * LANES, hid), BF16),
            pltpu.VMEM((2 * LANES, hid), BF16),
            pltpu.VMEM((2 * LANES, hid), BF16),
            pltpu.VMEM((chunks, rows, 2 * LANES), BF16),
            pltpu.VMEM((chunks, rows, 2 * LANES), BF16),
            *[pltpu.VMEM(shape.shape, BF16) for shape in shapes],
            dma((5,)),
            dma((5,)),
            dma,
            dma((chunks,)),
            dma,
            dma,
            dma((chunks, 4)),
            dma((chunks, 2, 2)),
            dma((chunks, 2)),
            dma((chunks, 2, 2)),
            dma((chunks, 2)),
            dma((chunks, 2, 3)),
            dma((chunks, 2, 3)),
        ],
        compiler_params=pltpu.CompilerParams(
            collective_id=0, has_side_effects=True, vmem_limit_bytes=60 * 1024 * 1024
        ),
    )(tokens.T, grad_out.T, expert_ids.T, gates.T, w_gate[0], w_up[0], w_down[0].T)
    mixed, grad_tokens, grad_gate, grad_up, grad_down = pl.pallas_call(
        deliver,
        out_shape=shapes,
        in_specs=[anywhere] * 5,
        out_specs=(anywhere,) * 5,
        scratch_shapes=[pltpu.VMEM(shape.shape, BF16) for shape in shapes] + [dma((5,)), dma((5,))],
    )(*results)
    return (mixed.T, grad_tokens.T, grad_gate[None], grad_up[None], grad_down.T[None])


def solution(mesh):
    placed = (
        P("expert", "dp"),
        P("expert", "dp"),
        P("expert", None),
        P("expert", None),
        P("expert", "dp", None),
        P("expert", "dp", None),
        P("expert", None, "dp"),
    )
    return jax.shard_map(
        body,
        mesh=mesh,
        in_specs=placed,
        out_specs=(
            P("expert", "dp"),
            P("expert", "dp"),
            P("expert", "dp", None),
            P("expert", "dp", None),
            P("expert", None, "dp"),
        ),
        check_vma=False,
    )
```

```python
import functools

import jax
import jax.numpy as jnp
from jax import lax
from jax.experimental import pallas as pl
from jax.experimental.pallas import tpu as pltpu
from jax.sharding import PartitionSpec as P

MESH = pl.DeviceIdType.MESH
BF16 = jnp.bfloat16
F32 = jnp.float32
RING = 4
STARTS = (0, 1, 4, 5, 7, 8, 11, 12)
LANES = 128


def dot(left, right, dims):
    return lax.dot_general(left, right, (dims, ((), ())), preferred_element_type=F32)


def z_wait(ref, sem):
    pltpu.make_async_copy(ref, ref, sem).wait()


def xy_wait(ref, sem):
    pltpu.make_async_copy(ref, ref, sem).wait()


def z_send(src, dst, send_sem, recv_sem, device):
    pltpu.make_async_remote_copy(src, dst, send_sem, recv_sem, device, MESH).start()


def xy_send_to(src, dst, send_sem, recv_sem, device):
    pltpu.make_async_remote_copy(src, dst, send_sem, recv_sem, device, MESH).start()


def kernel(
    experts,
    cap,
    chunks,
    tok_ref,
    gout_ref,
    ids_ref,
    gates_ref,
    wg_ref,
    wu_ref,
    wd_ref,
    mixed_ref,
    gtok_ref,
    ggate_ref,
    gup_ref,
    gdown_ref,
    send,
    recv,
    part,
    ra1,
    rb1,
    red,
    ra2,
    rb2,
    full,
    ret,
    back,
    place,
    comb,
    wgp,
    wup,
    wdp,
    xs,
    gs,
    out_m,
    out_t,
    out_g,
    out_u,
    out_d,
    in_sem,
    out_sem,
    disp_send,
    disp_recv,
    back_send,
    back_recv,
    xy_send,
    ra1_sem,
    rb1_sem,
    ra2_sem,
    rb2_sem,
    ag2_sem,
    ag1_sem,
):
    dp = lax.axis_index("dp")
    me = lax.axis_index("expert")
    px, py = dp // RING, dp % RING
    zs = experts // 2
    z, core = me // 2, me % 2
    per = zs // chunks
    blocks = 2 * per
    rows = blocks * cap
    feat, toks = tok_ref.shape
    slots = experts * cap
    col = part.shape[-1]
    q2 = red.shape[-2]

    def peer(dz, dc):
        return ((z + dz) % zs) * 2 + (core if dc == 0 else 1 - core)

    def x_peer(step):
        return ((px + step) % RING) * RING + py

    def y_peer(step):
        return px * RING + (py + step) % RING

    def distance(c, j):
        base = per * c
        if chunks == len(STARTS):
            late = c // (chunks // 2)
            base = 2 * per * ((1 - late) * c + late * (chunks - 1 - c)) + late * per
        k = base + j
        far, odd = (k + 1) // 2, k % 2
        return (odd * far + (1 - odd) * (zs - far)) % zs

    barrier = pltpu.get_barrier_semaphore()
    for dz in range(zs):
        for dc in range(2):
            if dz or dc:
                pl.semaphore_signal(
                    barrier, inc=1, device_id=(dp, peer(dz, dc)), device_id_type=MESH
                )
    for near in (x_peer(1), x_peer(RING - 1), y_peer(1), y_peer(RING - 1)):
        pl.semaphore_signal(barrier, inc=1, device_id=(near, me), device_id_type=MESH)

    wide = feat - LANES
    cut = 2 * LANES - wide
    pieces = (
        (wg_ref, wgp.at[0:feat]),
        (wu_ref, wup.at[0:feat]),
        (wd_ref.at[0:LANES], wdp.at[0:LANES]),
        (wd_ref.at[cut:feat], wdp.at[LANES : LANES + feat - cut]),
        (wd_ref.at[LANES:cut], wdp.at[LANES + wide : 2 * LANES]),
    )
    loads = [pltpu.make_async_copy(pair[0], pair[1], in_sem.at[i]) for i, pair in enumerate(pieces)]
    for load in loads:
        load.start()
    wgp[feat : 2 * LANES, :] = jnp.zeros((2 * LANES - feat, wgp.shape[1]), BF16)
    wup[feat : 2 * LANES, :] = jnp.zeros((2 * LANES - feat, wgp.shape[1]), BF16)
    wdp[LANES + feat - cut : LANES + wide, :] = jnp.zeros((wide + cut - feat, wgp.shape[1]), BF16)

    ids = ids_ref[...]
    inside = ids < experts
    chosen = jnp.sum(jnp.where(inside, ids, 0).astype(F32), axis=0, keepdims=True)
    routed = jnp.sum(jnp.where(inside, 1.0, 0.0), axis=0, keepdims=True)
    weight = jnp.sum(jnp.where(inside, gates_ref[...], 0.0), axis=0, keepdims=True)
    row_e = lax.broadcasted_iota(jnp.int32, (experts, toks), 0).astype(F32)
    one_hot = jnp.where((row_e == chosen) & (routed > 0.0), 1.0, 0.0)
    earlier = jnp.where(
        lax.broadcasted_iota(jnp.int32, (toks, toks), 0)
        < lax.broadcasted_iota(jnp.int32, (toks, toks), 1),
        1.0,
        0.0,
    ).astype(BF16)
    counts = dot(one_hot.astype(BF16), earlier, ((1,), (0,)))
    position = jnp.sum(counts * one_hot, axis=0, keepdims=True)
    slot = jnp.where(routed > 0.0, chosen * cap + position, 2.0 * slots)
    scaled = (weight * gout_ref[...].astype(F32)).astype(BF16)
    comb[0:LANES, :] = tok_ref[0:LANES, :]
    comb[LANES : 2 * LANES, :] = scaled[0:LANES, :]
    comb[2 * LANES : 2 * LANES + wide, :] = tok_ref[LANES:feat, :]
    comb[2 * LANES + wide : 3 * LANES, :] = scaled[LANES:cut, :]
    comb[3 * LANES : 3 * LANES + feat - cut, :] = scaled[cut:feat, :]
    comb[3 * LANES + feat - cut : 4 * LANES, :] = scaled[cut:feat, :]
    half = cap // 2
    lane = lax.broadcasted_iota(jnp.int32, (1, 1, LANES), 2)
    row = lax.broadcasted_iota(jnp.int32, (cap, toks), 0).astype(F32)

    def partner(c, k):
        return peer(zs - distance(c, k // 2), k % 2)

    def dispatch(low, high):
        for i in range(low * blocks, high * blocks):
            start = partner(i // blocks, i % blocks) * cap
            place[i * cap : (i + 1) * cap, :] = jnp.where(
                row == slot - start.astype(F32), 1.0, 0.0
            ).astype(BF16)
        count = (high - low) * blocks
        here = slice(low * blocks, high * blocks)
        laid = dot(place[low * rows : high * rows, :], comb[...], ((1,), (1,)))
        for i in range(3):
            send[here, i * cap : (i + 1) * cap, :] = (
                laid[:, i * LANES : (i + 1) * LANES].astype(BF16).reshape(count, cap, LANES)
            )
        last = laid[:, 3 * LANES : 4 * LANES].reshape(count, cap, LANES)
        send[here, 3 * cap : 3 * cap + half, :] = jnp.where(
            lane < LANES // 2, last[:, 0:half, :], last[:, half:cap, :]
        ).astype(BF16)
        if low == 0:
            pl.semaphore_wait(barrier, 2 * zs - 1 + 4)
        for c in range(low, high):
            for k in range(blocks):
                source, target = send.at[c * blocks + k], recv.at[c, k]
                if c == 0 and k == 0:
                    pltpu.make_async_copy(source, target, disp_recv.at[c]).start()
                else:
                    there = partner(c, k)
                    z_send(source, target, disp_send, disp_recv.at[c], (dp, there))

    near = min(2, chunks)
    dispatch(0, near)
    if near < chunks:
        dispatch(near, chunks)

    def unpack(rows3, count):
        first_x = rows3[:, 0:cap, :]
        first_g = rows3[:, cap : 2 * cap, :]
        both = rows3[:, 2 * cap : 3 * cap, :]
        pair = rows3[:, 3 * cap : 3 * cap + half, :].astype(F32)
        other = pltpu.roll(pair.reshape(count * half, LANES), LANES // 2, 1)
        pair = jnp.concatenate([pair, other.reshape(count, half, LANES)], axis=1)
        rest = jnp.where(
            lane < LANES // 2, pair, jnp.where(lane >= wide, both.astype(F32), 0.0)
        ).astype(BF16)
        n = count * cap
        return (
            (first_x.reshape(n, LANES), both.reshape(n, LANES)),
            (first_g.reshape(n, LANES), rest.reshape(n, LANES)),
        )

    for load in loads:
        load.wait()

    def hop(src, dst, send_sem, recv_sem, near):
        xy_send_to(src, dst, send_sem, recv_sem, (near, me))

    first = ((px, x_peer(1), x_peer(RING - 1)), (py, y_peer(1), y_peer(RING - 1)))
    second = (first[1], first[0])

    def rs_start(src, ra, rb, c, h, ring, ssem, ra_sem, rb_sem):
        p, right, left = ring
        lo, hi = 2 * h, 2 * h + 1
        hop(src.at[c, lo, (p + 2) % 4], ra.at[c, h, 0], ssem, ra_sem.at[c, h, 0], right)
        hop(src.at[c, hi, (p + 2) % 4], ra.at[c, h, 1], ssem, ra_sem.at[c, h, 1], left)
        hop(src.at[c, hi, (p + 1) % 4], rb.at[c, h, 0], ssem, rb_sem.at[c, h], right)
        hop(src.at[c, lo, (p + 3) % 4], rb.at[c, h, 1], ssem, rb_sem.at[c, h], left)

    def rs_relay(src, ra, rb, c, h, ring, ssem, ra_sem, rb_sem):
        p, right, left = ring
        for side, b, t, near in ((0, 2 * h, (p + 1) % 4, right), (1, 2 * h + 1, (p + 3) % 4, left)):
            xy_wait(ra.at[c, h, side], ra_sem.at[c, h, side])
            src[c, b, t] = (src[c, b, t].astype(F32) + ra[c, h, side].astype(F32)).astype(BF16)
            hop(src.at[c, b, t], rb.at[c, h, 2 + side], ssem, rb_sem.at[c, h], near)

    def rs_final(src, rb, c, h, ring, rb_sem):
        p = ring[0]
        xy_wait(rb.at[c, h], rb_sem.at[c, h])
        lo = src[c, 2 * h, p].astype(F32) + rb[c, h, 1].astype(F32) + rb[c, h, 2].astype(F32)
        hi = src[c, 2 * h + 1, p].astype(F32) + rb[c, h, 0].astype(F32) + rb[c, h, 3].astype(F32)
        return lo, hi

    def stage_partials(c):
        z_wait(recv.at[c], disp_recv.at[c])
        x_pair, g_pair = unpack(recv[c], blocks)
        for i in range(2):
            xs[c, :, i * LANES : (i + 1) * LANES] = x_pair[i]
            gs[c, :, i * LANES : (i + 1) * LANES] = g_pair[i]
        x = xs[c]
        g = gs[c]
        for h in range(2):
            for b in (2 * h, 2 * h + 1):
                cols = slice(b * col, (b + 1) * col)
                terms = (
                    dot(x, wgp[:, cols], ((1,), (0,))),
                    dot(x, wup[:, cols], ((1,), (0,))),
                    dot(g, wdp[:, cols], ((1,), (0,))),
                )
                for a in range(3):
                    part[c, b, :, a] = terms[a].astype(BF16).reshape(4, rows // 4, col)
            rs_start(part, ra1, rb1, c, h, first[h], xy_send.at[c, 0], ra1_sem, rb1_sem)

    def stage_relay1(c):
        for h in range(2):
            rs_relay(part, ra1, rb1, c, h, first[h], xy_send.at[c, 0], ra1_sem, rb1_sem)

    def stage_second(c):
        for h in range(2):
            sums = rs_final(part, rb1, c, h, first[h], rb1_sem)
            for side in range(2):
                for a in range(3):
                    red[c, 2 * h + side, :, a] = sums[side][a].astype(BF16).reshape(4, q2, col)
            rs_start(red, ra2, rb2, c, h, second[h], xy_send.at[c, 1], ra2_sem, rb2_sem)

    def stage_relay2(c):
        for h in range(2):
            rs_relay(red, ra2, rb2, c, h, second[h], xy_send.at[c, 1], ra2_sem, rb2_sem)

    def stage_pointwise(c):
        for h in range(2):
            p1 = first[h][0]
            p2, right, left = second[h]
            sums = rs_final(red, rb2, c, h, second[h], rb2_sem)
            for side in range(2):
                gate, up, grad = sums[side][0], sums[side][1], sums[side][2]
                logistic = 1.0 / (1.0 + jnp.exp(-gate))
                swish = gate * logistic
                full[c, h, p1, p2, side, 0] = (swish * up).astype(BF16)
                full[c, h, p1, p2, side, 1] = (
                    grad * up * (logistic * (1.0 + gate * (1.0 - logistic)))
                ).astype(BF16)
                full[c, h, p1, p2, side, 2] = (grad * swish).astype(BF16)
            own = full.at[c, h, p1, p2]
            hop(own, own, xy_send.at[c, 2], ag2_sem.at[c, h, 0], right)
            hop(own, own, xy_send.at[c, 2], ag2_sem.at[c, h, 1], left)

    def stage_forward2(c):
        for h in range(2):
            p1 = first[h][0]
            p2, right, left = second[h]
            for side, t, near in ((0, (p2 + 3) % 4, right), (1, (p2 + 1) % 4, left)):
                xy_wait(full.at[c, h, p1, t], ag2_sem.at[c, h, side])
                piece = full.at[c, h, p1, t, side]
                hop(piece, piece, xy_send.at[c, 2], ag2_sem.at[c, h, 2], near)

    def stage_first(c):
        for h in range(2):
            p1, right, left = first[h]
            p2 = second[h][0]
            xy_wait(full.at[c, h, p1, (p2 + 2) % 4], ag2_sem.at[c, h, 2])
            own = full.at[c, h, p1]
            hop(own, own, xy_send.at[c, 3], ag1_sem.at[c, h, 0], right)
            hop(own, own, xy_send.at[c, 3], ag1_sem.at[c, h, 1], left)

    def stage_forward1(c):
        for h in range(2):
            p1, right, left = first[h]
            for side, t, near in ((0, (p1 + 3) % 4, right), (1, (p1 + 1) % 4, left)):
                xy_wait(full.at[c, h, t], ag1_sem.at[c, h, side])
                piece = full.at[c, h, t, :, side]
                hop(piece, piece, xy_send.at[c, 3], ag1_sem.at[c, h, 2], near)

    def stage_outputs(c):
        for h in range(2):
            xy_wait(full.at[c, h, (first[h][0] + 2) % 4], ag1_sem.at[c, h, 2])
        out = jnp.zeros((rows, 2 * LANES), F32)
        grad = jnp.zeros((rows, 2 * LANES), F32)
        for b in range(4):
            cols = slice(b * col, (b + 1) * col)
            act, dgate, dup = (
                full[c, b // 2, :, :, b % 2, a].reshape(rows, col) for a in range(3)
            )
            out += dot(act, wdp[:, cols], ((1,), (1,)))
            grad += dot(dgate, wgp[:, cols], ((1,), (1,)))
            grad += dot(dup, wup[:, cols], ((1,), (1,)))
        packed = (blocks, cap, LANES)
        rest = out[:, LANES : 2 * LANES].reshape(packed)
        turned = pltpu.roll(rest[:, half:cap, :].reshape(blocks * half, LANES), LANES // 2, 1)
        ret[c, :, 0:cap, :] = grad[:, 0:LANES].astype(BF16).reshape(packed)
        ret[c, :, cap : 2 * cap, :] = out[:, 0:LANES].astype(BF16).reshape(packed)
        ret[c, :, 2 * cap : 3 * cap, :] = jnp.where(
            lane < wide, grad[:, LANES : 2 * LANES].reshape(packed), rest
        ).astype(BF16)
        ret[c, :, 3 * cap : 3 * cap + half, :] = jnp.where(
            lane < LANES // 2, rest[:, 0:half, :], turned.reshape(blocks, half, LANES)
        ).astype(BF16)

        def go(k):
            there = peer(distance(c, k // 2), k % 2)
            z_send(ret.at[c, k], back.at[c * blocks + k], back_send, back_recv.at[c], (dp, there))

        @pl.when(c == 0)
        def _():
            pltpu.make_async_copy(ret.at[c, 0], back.at[0], back_recv.at[c]).start()

        @pl.when(c > 0)
        def _():
            go(0)

        for k in range(1, blocks):
            go(k)

    stages = (
        stage_partials,
        stage_relay1,
        stage_second,
        stage_relay2,
        stage_pointwise,
        stage_forward2,
        stage_first,
        stage_forward1,
        stage_outputs,
    )

    starts = STARTS[:chunks]

    def step(t, carry):
        for s in reversed(range(len(stages))):
            since = t - s
            c = sum((since >= begin).astype(jnp.int32) for begin in starts[1:])

            @pl.when(functools.reduce(jnp.logical_or, [since == begin for begin in starts]))
            def _(s=s, c=c):
                stages[s](c)

        return carry

    lax.fori_loop(0, len(stages) + starts[-1], step, 0)

    def restore(ref, value):
        ref[0:LANES, :] = value[0:LANES].astype(BF16)
        ref[LANES:cut, :] = value[LANES + wide : 2 * LANES].astype(BF16)
        ref[cut:feat, :] = value[LANES : LANES + feat - cut].astype(BF16)

    x_t = xs[...].reshape(slots, 2 * LANES).T
    g_t = gs[...].reshape(slots, 2 * LANES).T
    for b in range(4):
        cols = slice(b * col, (b + 1) * col)
        act, dgate, dup = (
            full[:, b // 2, :, :, b % 2, a].reshape(slots, col) for a in range(3)
        )
        out_g[:, cols] = dot(x_t, dgate, ((1,), (0,)))[0:feat].astype(BF16)
        out_u[:, cols] = dot(x_t, dup, ((1,), (0,)))[0:feat].astype(BF16)
        restore(out_d.at[:, cols], dot(g_t, act, ((1,), (0,))))

    def leave(i, src, dst):
        out = pltpu.make_async_copy(src, dst, out_sem.at[i])
        out.start()
        return out

    outs = [leave(0, out_g, ggate_ref), leave(1, out_u, gup_ref), leave(2, out_d, gdown_ref)]

    spots = ((0,), (0,))
    early = max(chunks - 2, 1)
    totals = []
    for low, high in ((0, early), (early, chunks)):
        for c in range(low, high):
            z_wait(back.at[c * blocks : (c + 1) * blocks], back_recv.at[c])
        grad_pair, out_pair = unpack(back[low * blocks : high * blocks], (high - low) * blocks)
        spot = place[low * rows : high * rows, :]
        totals.append(
            (
                dot(jnp.concatenate(out_pair, axis=1), spot, spots),
                dot(jnp.concatenate(grad_pair, axis=1), spot, spots),
            )
        )
    restore(out_m, weight * (totals[0][0] + totals[1][0]))
    outs.append(leave(3, out_m, mixed_ref))
    out_t[...] = (totals[0][1] + totals[1][1])[0:feat].astype(BF16)
    outs.append(leave(4, out_t, gtok_ref))

    z_wait(send.at[0 : experts - 1], disp_send)
    z_wait(back.at[0 : experts - 1], back_send)
    for c in range(chunks):
        xy_wait(part.at[c, 0:3], xy_send.at[c, 0])
        xy_wait(red.at[c, 0:3], xy_send.at[c, 1])
        xy_wait(full.at[c, :, 0, 0:3], xy_send.at[c, 2])
        xy_wait(full.at[c, :, 0:3], xy_send.at[c, 3])
    for out in outs:
        out.wait()


def deliver(*refs):
    sources, targets, held = refs[0:5], refs[5:10], refs[10:15]
    in_sem, out_sem = refs[15:17]
    ins = [pltpu.make_async_copy(sources[i], held[i], in_sem.at[i]) for i in range(5)]
    outs = [pltpu.make_async_copy(held[i], targets[i], out_sem.at[i]) for i in range(5)]
    for copy in ins:
        copy.start()
    for i in range(5):
        ins[i].wait()
        outs[i].start()
    for copy in outs:
        copy.wait()


def body(tokens, grad_out, expert_ids, gates, w_gate, w_up, w_down):
    experts = lax.axis_size("expert")
    toks, feat = tokens.shape
    hid = w_gate.shape[-1]
    cap = toks // 16
    zs = experts // 2
    chunks = min(len(STARTS), zs)
    rows = experts * cap // chunks
    q1, q2, col = rows // 4, rows // 16, hid // 4
    packed = 3 * cap + cap // 2
    dma = pltpu.SemaphoreType.DMA
    shapes = (
        jax.ShapeDtypeStruct((feat, toks), BF16),
        jax.ShapeDtypeStruct((feat, toks), BF16),
        jax.ShapeDtypeStruct((feat, hid), BF16),
        jax.ShapeDtypeStruct((feat, hid), BF16),
        jax.ShapeDtypeStruct((feat, hid), BF16),
    )
    anywhere = pl.BlockSpec(memory_space=pl.ANY)
    results = pl.pallas_call(
        functools.partial(kernel, experts, cap, chunks),
        out_shape=shapes,
        in_specs=[pl.BlockSpec(memory_space=pltpu.VMEM)] * 4 + [anywhere] * 3,
        out_specs=(anywhere,) * 5,
        scratch_shapes=[
            pltpu.VMEM((experts, packed, LANES), BF16),
            pltpu.VMEM((chunks, experts // chunks, packed, LANES), BF16),
            pltpu.VMEM((chunks, 4, 4, 3, q1, col), BF16),
            pltpu.VMEM((chunks, 2, 2, 3, q1, col), BF16),
            pltpu.VMEM((chunks, 2, 4, 3, q1, col), BF16),
            pltpu.VMEM((chunks, 4, 4, 3, q2, col), BF16),
            pltpu.VMEM((chunks, 2, 2, 3, q2, col), BF16),
            pltpu.VMEM((chunks, 2, 4, 3, q2, col), BF16),
            pltpu.VMEM((chunks, 2, 4, 4, 2, 3, q2, col), BF16),
            pltpu.VMEM((chunks, experts // chunks, packed, LANES), BF16),
            pltpu.VMEM((experts, packed, LANES), BF16),
            pltpu.VMEM((experts * cap, toks), BF16),
            pltpu.VMEM((4 * LANES, toks), BF16),
            pltpu.VMEM((2 * LANES, hid), BF16),
            pltpu.VMEM((2 * LANES, hid), BF16),
            pltpu.VMEM((2 * LANES, hid), BF16),
            pltpu.VMEM((chunks, rows, 2 * LANES), BF16),
            pltpu.VMEM((chunks, rows, 2 * LANES), BF16),
            *[pltpu.VMEM(shape.shape, BF16) for shape in shapes],
            dma((5,)),
            dma((5,)),
            dma,
            dma((chunks,)),
            dma,
            dma((chunks,)),
            dma((chunks, 4)),
            dma((chunks, 2, 2)),
            dma((chunks, 2)),
            dma((chunks, 2, 2)),
            dma((chunks, 2)),
            dma((chunks, 2, 3)),
            dma((chunks, 2, 3)),
        ],
        compiler_params=pltpu.CompilerParams(
            collective_id=0, has_side_effects=True, vmem_limit_bytes=60 * 1024 * 1024
        ),
    )(tokens.T, grad_out.T, expert_ids.T, gates.T, w_gate[0], w_up[0], w_down[0].T)
    mixed, grad_tokens, grad_gate, grad_up, grad_down = pl.pallas_call(
        deliver,
        out_shape=shapes,
        in_specs=[anywhere] * 5,
        out_specs=(anywhere,) * 5,
        scratch_shapes=[pltpu.VMEM(shape.shape, BF16) for shape in shapes] + [dma((5,)), dma((5,))],
    )(*results)
    return (mixed.T, grad_tokens.T, grad_gate[None], grad_up[None], grad_down.T[None])


def solution(mesh):
    placed = (
        P("expert", "dp"),
        P("expert", "dp"),
        P("expert", None),
        P("expert", None),
        P("expert", "dp", None),
        P("expert", "dp", None),
        P("expert", None, "dp"),
    )
    return jax.shard_map(
        body,
        mesh=mesh,
        in_specs=placed,
        out_specs=(
            P("expert", "dp"),
            P("expert", "dp"),
            P("expert", "dp", None),
            P("expert", "dp", None),
            P("expert", None, "dp"),
        ),
        check_vma=False,
    )
```

```python
import functools

import jax
import jax.numpy as jnp
from jax import lax
from jax.experimental import pallas as pl
from jax.experimental.pallas import tpu as pltpu
from jax.sharding import PartitionSpec as P

MESH = pl.DeviceIdType.MESH
BF16 = jnp.bfloat16
F32 = jnp.float32
RING = 4
STARTS = (0, 1, 4, 5, 7, 8, 11, 12)
LANES = 128
NEARNESS = (0, 1, 3, 5, 7, 6, 4, 2)


def dot(left, right, dims):
    return lax.dot_general(left, right, (dims, ((), ())), preferred_element_type=F32)


def pick_from(table, index):
    if isinstance(index, int):
        return table[index]
    return sum((index == i).astype(jnp.int32) * value for i, value in enumerate(table))


def z_wait(ref, sem):
    pltpu.make_async_copy(ref, ref, sem).wait()


def xy_wait(ref, sem):
    pltpu.make_async_copy(ref, ref, sem).wait()


def z_send(src, dst, send_sem, recv_sem, device):
    pltpu.make_async_remote_copy(src, dst, send_sem, recv_sem, device, MESH).start()


def xy_send_to(src, dst, send_sem, recv_sem, device):
    pltpu.make_async_remote_copy(src, dst, send_sem, recv_sem, device, MESH).start()


def kernel(
    experts,
    cap,
    chunks,
    tok_ref,
    gout_ref,
    ids_ref,
    gates_ref,
    wg_ref,
    wu_ref,
    wd_ref,
    mixed_ref,
    gtok_ref,
    ggate_ref,
    gup_ref,
    gdown_ref,
    send,
    recv,
    part,
    ra1,
    rb1,
    red,
    ra2,
    rb2,
    full,
    ret,
    back,
    place,
    comb,
    wgp,
    wup,
    wdp,
    xs,
    gs,
    out_m,
    out_t,
    out_g,
    out_u,
    out_d,
    in_sem,
    out_sem,
    disp_send,
    disp_recv,
    back_send,
    back_recv,
    xy_send,
    ra1_sem,
    rb1_sem,
    ra2_sem,
    rb2_sem,
    ag2_sem,
    ag1_sem,
):
    dp = lax.axis_index("dp")
    me = lax.axis_index("expert")
    px, py = dp // RING, dp % RING
    zs = experts // 2
    z, core = me // 2, me % 2
    per = zs // chunks
    blocks = 2 * per
    rows = blocks * cap
    feat, toks = tok_ref.shape
    slots = experts * cap
    col = part.shape[-1]
    q2 = red.shape[-2]

    def peer(dz, dc):
        return ((z + dz) % zs) * 2 + (core if dc == 0 else 1 - core)

    def x_peer(step):
        return ((px + step) % RING) * RING + py

    def y_peer(step):
        return px * RING + (py + step) % RING

    def distance(c, j):
        base = per * c
        if chunks == len(STARTS):
            base = per * pick_from(NEARNESS, c)
        k = base + j
        far, odd = (k + 1) // 2, k % 2
        return (odd * far + (1 - odd) * (zs - far)) % zs

    barrier = pltpu.get_barrier_semaphore()
    for dz in range(zs):
        for dc in range(2):
            if dz or dc:
                pl.semaphore_signal(
                    barrier, inc=1, device_id=(dp, peer(dz, dc)), device_id_type=MESH
                )
    for near in (x_peer(1), x_peer(RING - 1), y_peer(1), y_peer(RING - 1)):
        pl.semaphore_signal(barrier, inc=1, device_id=(near, me), device_id_type=MESH)

    wide = feat - LANES
    cut = 2 * LANES - wide
    pieces = (
        (wg_ref, wgp.at[0:feat]),
        (wu_ref, wup.at[0:feat]),
        (wd_ref.at[0:LANES], wdp.at[0:LANES]),
        (wd_ref.at[cut:feat], wdp.at[LANES : LANES + feat - cut]),
        (wd_ref.at[LANES:cut], wdp.at[LANES + wide : 2 * LANES]),
    )
    loads = [pltpu.make_async_copy(pair[0], pair[1], in_sem.at[i]) for i, pair in enumerate(pieces)]
    for load in loads:
        load.start()
    wgp[feat : 2 * LANES, :] = jnp.zeros((2 * LANES - feat, wgp.shape[1]), BF16)
    wup[feat : 2 * LANES, :] = jnp.zeros((2 * LANES - feat, wgp.shape[1]), BF16)
    wdp[LANES + feat - cut : LANES + wide, :] = jnp.zeros((wide + cut - feat, wgp.shape[1]), BF16)

    ids = ids_ref[...]
    inside = ids < experts
    chosen = jnp.sum(jnp.where(inside, ids, 0).astype(F32), axis=0, keepdims=True)
    routed = jnp.sum(jnp.where(inside, 1.0, 0.0), axis=0, keepdims=True)
    weight = jnp.sum(jnp.where(inside, gates_ref[...], 0.0), axis=0, keepdims=True)
    row_e = lax.broadcasted_iota(jnp.int32, (experts, toks), 0).astype(F32)
    one_hot = jnp.where((row_e == chosen) & (routed > 0.0), 1.0, 0.0)
    earlier = jnp.where(
        lax.broadcasted_iota(jnp.int32, (toks, toks), 0)
        < lax.broadcasted_iota(jnp.int32, (toks, toks), 1),
        1.0,
        0.0,
    ).astype(BF16)
    counts = dot(one_hot.astype(BF16), earlier, ((1,), (0,)))
    position = jnp.sum(counts * one_hot, axis=0, keepdims=True)
    slot = jnp.where(routed > 0.0, chosen * cap + position, 2.0 * slots)
    scaled = (weight * gout_ref[...].astype(F32)).astype(BF16)
    comb[0:LANES, :] = tok_ref[0:LANES, :]
    comb[LANES : 2 * LANES, :] = scaled[0:LANES, :]
    comb[2 * LANES : 2 * LANES + wide, :] = tok_ref[LANES:feat, :]
    comb[2 * LANES + wide : 3 * LANES, :] = scaled[LANES:cut, :]
    comb[3 * LANES : 3 * LANES + feat - cut, :] = scaled[cut:feat, :]
    comb[3 * LANES + feat - cut : 4 * LANES, :] = scaled[cut:feat, :]
    half = cap // 2
    lane = lax.broadcasted_iota(jnp.int32, (1, 1, LANES), 2)
    row = lax.broadcasted_iota(jnp.int32, (cap, toks), 0).astype(F32)

    def partner(c, k):
        return peer(zs - distance(c, k // 2), k % 2)

    def dispatch(low, high):
        for i in range(low * blocks, high * blocks):
            start = partner(i // blocks, i % blocks) * cap
            place[i * cap : (i + 1) * cap, :] = jnp.where(
                row == slot - start.astype(F32), 1.0, 0.0
            ).astype(BF16)
        count = (high - low) * blocks
        here = slice(low * blocks, high * blocks)
        laid = dot(place[low * rows : high * rows, :], comb[...], ((1,), (1,)))
        for i in range(3):
            send[here, i * cap : (i + 1) * cap, :] = (
                laid[:, i * LANES : (i + 1) * LANES].astype(BF16).reshape(count, cap, LANES)
            )
        last = laid[:, 3 * LANES : 4 * LANES].reshape(count, cap, LANES)
        send[here, 3 * cap : 3 * cap + half, :] = jnp.where(
            lane < LANES // 2, last[:, 0:half, :], last[:, half:cap, :]
        ).astype(BF16)
        if low == 0:
            pl.semaphore_wait(barrier, 2 * zs - 1 + 4)
        for c in range(low, high):
            for k in range(blocks):
                source, target = send.at[c * blocks + k], recv.at[c, k]
                if c == 0 and k == 0:
                    pltpu.make_async_copy(source, target, disp_recv.at[c]).start()
                else:
                    there = partner(c, k)
                    z_send(source, target, disp_send, disp_recv.at[c], (dp, there))

    near = min(2, chunks)
    dispatch(0, near)
    if near < chunks:
        dispatch(near, chunks)

    def unpack(rows3, count):
        first_x = rows3[:, 0:cap, :]
        first_g = rows3[:, cap : 2 * cap, :]
        both = rows3[:, 2 * cap : 3 * cap, :]
        pair = rows3[:, 3 * cap : 3 * cap + half, :].astype(F32)
        other = pltpu.roll(pair.reshape(count * half, LANES), LANES // 2, 1)
        pair = jnp.concatenate([pair, other.reshape(count, half, LANES)], axis=1)
        rest = jnp.where(
            lane < LANES // 2, pair, jnp.where(lane >= wide, both.astype(F32), 0.0)
        ).astype(BF16)
        n = count * cap
        return (
            (first_x.reshape(n, LANES), both.reshape(n, LANES)),
            (first_g.reshape(n, LANES), rest.reshape(n, LANES)),
        )

    for load in loads:
        load.wait()

    def hop(src, dst, send_sem, recv_sem, near):
        xy_send_to(src, dst, send_sem, recv_sem, (near, me))

    first = ((px, x_peer(1), x_peer(RING - 1)), (py, y_peer(1), y_peer(RING - 1)))
    second = (first[1], first[0])

    def rs_start(src, ra, rb, c, h, ring, ssem, ra_sem, rb_sem):
        p, right, left = ring
        lo, hi = 2 * h, 2 * h + 1
        hop(src.at[c, lo, (p + 2) % 4], ra.at[c, h, 0], ssem, ra_sem.at[c, h, 0], right)
        hop(src.at[c, hi, (p + 2) % 4], ra.at[c, h, 1], ssem, ra_sem.at[c, h, 1], left)
        hop(src.at[c, hi, (p + 1) % 4], rb.at[c, h, 0], ssem, rb_sem.at[c, h], right)
        hop(src.at[c, lo, (p + 3) % 4], rb.at[c, h, 1], ssem, rb_sem.at[c, h], left)

    def rs_relay(src, ra, rb, c, h, ring, ssem, ra_sem, rb_sem):
        p, right, left = ring
        for side, b, t, near in ((0, 2 * h, (p + 1) % 4, right), (1, 2 * h + 1, (p + 3) % 4, left)):
            xy_wait(ra.at[c, h, side], ra_sem.at[c, h, side])
            src[c, b, t] = (src[c, b, t].astype(F32) + ra[c, h, side].astype(F32)).astype(BF16)
            hop(src.at[c, b, t], rb.at[c, h, 2 + side], ssem, rb_sem.at[c, h], near)

    def rs_final(src, rb, c, h, ring, rb_sem):
        p = ring[0]
        xy_wait(rb.at[c, h], rb_sem.at[c, h])
        lo = src[c, 2 * h, p].astype(F32) + rb[c, h, 1].astype(F32) + rb[c, h, 2].astype(F32)
        hi = src[c, 2 * h + 1, p].astype(F32) + rb[c, h, 0].astype(F32) + rb[c, h, 3].astype(F32)
        return lo, hi

    def stage_partials(c):
        z_wait(recv.at[c], disp_recv.at[c])
        x_pair, g_pair = unpack(recv[c], blocks)
        for i in range(2):
            xs[c, :, i * LANES : (i + 1) * LANES] = x_pair[i]
            gs[c, :, i * LANES : (i + 1) * LANES] = g_pair[i]
        x = xs[c]
        g = gs[c]
        for h in range(2):
            for b in (2 * h, 2 * h + 1):
                cols = slice(b * col, (b + 1) * col)
                terms = (
                    dot(x, wgp[:, cols], ((1,), (0,))),
                    dot(x, wup[:, cols], ((1,), (0,))),
                    dot(g, wdp[:, cols], ((1,), (0,))),
                )
                for a in range(3):
                    part[c, b, :, a] = terms[a].astype(BF16).reshape(4, rows // 4, col)
            rs_start(part, ra1, rb1, c, h, first[h], xy_send.at[c, 0], ra1_sem, rb1_sem)

    def stage_relay1(c):
        for h in range(2):
            rs_relay(part, ra1, rb1, c, h, first[h], xy_send.at[c, 0], ra1_sem, rb1_sem)

    def stage_second(c):
        for h in range(2):
            sums = rs_final(part, rb1, c, h, first[h], rb1_sem)
            for side in range(2):
                for a in range(3):
                    red[c, 2 * h + side, :, a] = sums[side][a].astype(BF16).reshape(4, q2, col)
            rs_start(red, ra2, rb2, c, h, second[h], xy_send.at[c, 1], ra2_sem, rb2_sem)

    def stage_relay2(c):
        for h in range(2):
            rs_relay(red, ra2, rb2, c, h, second[h], xy_send.at[c, 1], ra2_sem, rb2_sem)

    def stage_pointwise(c):
        for h in range(2):
            p1 = first[h][0]
            p2, right, left = second[h]
            sums = rs_final(red, rb2, c, h, second[h], rb2_sem)
            for side in range(2):
                gate, up, grad = sums[side][0], sums[side][1], sums[side][2]
                logistic = 1.0 / (1.0 + jnp.exp(-gate))
                swish = gate * logistic
                full[c, h, p1, p2, side, 0] = (swish * up).astype(BF16)
                full[c, h, p1, p2, side, 1] = (
                    grad * up * (logistic * (1.0 + gate * (1.0 - logistic)))
                ).astype(BF16)
                full[c, h, p1, p2, side, 2] = (grad * swish).astype(BF16)
            own = full.at[c, h, p1, p2]
            hop(own, own, xy_send.at[c, 2], ag2_sem.at[c, h, 0], right)
            hop(own, own, xy_send.at[c, 2], ag2_sem.at[c, h, 1], left)

    def stage_forward2(c):
        for h in range(2):
            p1 = first[h][0]
            p2, right, left = second[h]
            for side, t, near in ((0, (p2 + 3) % 4, right), (1, (p2 + 1) % 4, left)):
                xy_wait(full.at[c, h, p1, t], ag2_sem.at[c, h, side])
                piece = full.at[c, h, p1, t, side]
                hop(piece, piece, xy_send.at[c, 2], ag2_sem.at[c, h, 2], near)

    def stage_first(c):
        for h in range(2):
            p1, right, left = first[h]
            p2 = second[h][0]
            xy_wait(full.at[c, h, p1, (p2 + 2) % 4], ag2_sem.at[c, h, 2])
            own = full.at[c, h, p1]
            hop(own, own, xy_send.at[c, 3], ag1_sem.at[c, h, 0], right)
            hop(own, own, xy_send.at[c, 3], ag1_sem.at[c, h, 1], left)

    def stage_forward1(c):
        for h in range(2):
            p1, right, left = first[h]
            for side, t, near in ((0, (p1 + 3) % 4, right), (1, (p1 + 1) % 4, left)):
                xy_wait(full.at[c, h, t], ag1_sem.at[c, h, side])
                piece = full.at[c, h, t, :, side]
                hop(piece, piece, xy_send.at[c, 3], ag1_sem.at[c, h, 2], near)

    def stage_outputs(c):
        for h in range(2):
            xy_wait(full.at[c, h, (first[h][0] + 2) % 4], ag1_sem.at[c, h, 2])
        out = jnp.zeros((rows, 2 * LANES), F32)
        grad = jnp.zeros((rows, 2 * LANES), F32)
        for b in range(4):
            cols = slice(b * col, (b + 1) * col)
            act, dgate, dup = (
                full[c, b // 2, :, :, b % 2, a].reshape(rows, col) for a in range(3)
            )
            out += dot(act, wdp[:, cols], ((1,), (1,)))
            grad += dot(dgate, wgp[:, cols], ((1,), (1,)))
            grad += dot(dup, wup[:, cols], ((1,), (1,)))
        packed = (blocks, cap, LANES)
        rest = out[:, LANES : 2 * LANES].reshape(packed)
        turned = pltpu.roll(rest[:, half:cap, :].reshape(blocks * half, LANES), LANES // 2, 1)
        ret[c, :, 0:cap, :] = grad[:, 0:LANES].astype(BF16).reshape(packed)
        ret[c, :, cap : 2 * cap, :] = out[:, 0:LANES].astype(BF16).reshape(packed)
        ret[c, :, 2 * cap : 3 * cap, :] = jnp.where(
            lane < wide, grad[:, LANES : 2 * LANES].reshape(packed), rest
        ).astype(BF16)
        ret[c, :, 3 * cap : 3 * cap + half, :] = jnp.where(
            lane < LANES // 2, rest[:, 0:half, :], turned.reshape(blocks, half, LANES)
        ).astype(BF16)

        def go(k):
            there = peer(distance(c, k // 2), k % 2)
            z_send(ret.at[c, k], back.at[c * blocks + k], back_send, back_recv.at[c], (dp, there))

        @pl.when(c == 0)
        def _():
            pltpu.make_async_copy(ret.at[c, 0], back.at[0], back_recv.at[c]).start()

        @pl.when(c > 0)
        def _():
            go(0)

        for k in range(1, blocks):
            go(k)

    stages = (
        stage_partials,
        stage_relay1,
        stage_second,
        stage_relay2,
        stage_pointwise,
        stage_forward2,
        stage_first,
        stage_forward1,
        stage_outputs,
    )

    starts = STARTS[:chunks]

    def step(t, carry):
        for s in reversed(range(len(stages))):
            since = t - s
            c = sum((since >= begin).astype(jnp.int32) for begin in starts[1:])

            @pl.when(functools.reduce(jnp.logical_or, [since == begin for begin in starts]))
            def _(s=s, c=c):
                stages[s](c)

        return carry

    lax.fori_loop(0, len(stages) + starts[-1], step, 0)

    def restore(ref, value):
        ref[0:LANES, :] = value[0:LANES].astype(BF16)
        ref[LANES:cut, :] = value[LANES + wide : 2 * LANES].astype(BF16)
        ref[cut:feat, :] = value[LANES : LANES + feat - cut].astype(BF16)

    x_t = xs[...].reshape(slots, 2 * LANES).T
    g_t = gs[...].reshape(slots, 2 * LANES).T
    for b in range(4):
        cols = slice(b * col, (b + 1) * col)
        act, dgate, dup = (
            full[:, b // 2, :, :, b % 2, a].reshape(slots, col) for a in range(3)
        )
        out_g[:, cols] = dot(x_t, dgate, ((1,), (0,)))[0:feat].astype(BF16)
        out_u[:, cols] = dot(x_t, dup, ((1,), (0,)))[0:feat].astype(BF16)
        restore(out_d.at[:, cols], dot(g_t, act, ((1,), (0,))))

    def leave(i, src, dst):
        out = pltpu.make_async_copy(src, dst, out_sem.at[i])
        out.start()
        return out

    outs = [leave(0, out_g, ggate_ref), leave(1, out_u, gup_ref), leave(2, out_d, gdown_ref)]

    spots = ((0,), (0,))
    early = max(chunks - 2, 1)
    totals = []
    for low, high in ((0, early), (early, chunks)):
        for c in range(low, high):
            z_wait(back.at[c * blocks : (c + 1) * blocks], back_recv.at[c])
        grad_pair, out_pair = unpack(back[low * blocks : high * blocks], (high - low) * blocks)
        spot = place[low * rows : high * rows, :]
        totals.append(
            (
                dot(jnp.concatenate(out_pair, axis=1), spot, spots),
                dot(jnp.concatenate(grad_pair, axis=1), spot, spots),
            )
        )
    restore(out_m, weight * (totals[0][0] + totals[1][0]))
    outs.append(leave(3, out_m, mixed_ref))
    out_t[...] = (totals[0][1] + totals[1][1])[0:feat].astype(BF16)
    outs.append(leave(4, out_t, gtok_ref))

    z_wait(send.at[0 : experts - 1], disp_send)
    z_wait(back.at[0 : experts - 1], back_send)
    for c in range(chunks):
        xy_wait(part.at[c, 0:3], xy_send.at[c, 0])
        xy_wait(red.at[c, 0:3], xy_send.at[c, 1])
        xy_wait(full.at[c, :, 0, 0:3], xy_send.at[c, 2])
        xy_wait(full.at[c, :, 0:3], xy_send.at[c, 3])
    for out in outs:
        out.wait()


def deliver(*refs):
    sources, targets, held = refs[0:5], refs[5:10], refs[10:15]
    in_sem, out_sem = refs[15:17]
    ins = [pltpu.make_async_copy(sources[i], held[i], in_sem.at[i]) for i in range(5)]
    outs = [pltpu.make_async_copy(held[i], targets[i], out_sem.at[i]) for i in range(5)]
    for copy in ins:
        copy.start()
    for i in range(5):
        ins[i].wait()
        outs[i].start()
    for copy in outs:
        copy.wait()


def body(tokens, grad_out, expert_ids, gates, w_gate, w_up, w_down):
    experts = lax.axis_size("expert")
    toks, feat = tokens.shape
    hid = w_gate.shape[-1]
    cap = toks // 16
    zs = experts // 2
    chunks = min(len(STARTS), zs)
    rows = experts * cap // chunks
    q1, q2, col = rows // 4, rows // 16, hid // 4
    packed = 3 * cap + cap // 2
    dma = pltpu.SemaphoreType.DMA
    shapes = (
        jax.ShapeDtypeStruct((feat, toks), BF16),
        jax.ShapeDtypeStruct((feat, toks), BF16),
        jax.ShapeDtypeStruct((feat, hid), BF16),
        jax.ShapeDtypeStruct((feat, hid), BF16),
        jax.ShapeDtypeStruct((feat, hid), BF16),
    )
    anywhere = pl.BlockSpec(memory_space=pl.ANY)
    results = pl.pallas_call(
        functools.partial(kernel, experts, cap, chunks),
        out_shape=shapes,
        in_specs=[pl.BlockSpec(memory_space=pltpu.VMEM)] * 4 + [anywhere] * 3,
        out_specs=(anywhere,) * 5,
        scratch_shapes=[
            pltpu.VMEM((experts, packed, LANES), BF16),
            pltpu.VMEM((chunks, experts // chunks, packed, LANES), BF16),
            pltpu.VMEM((chunks, 4, 4, 3, q1, col), BF16),
            pltpu.VMEM((chunks, 2, 2, 3, q1, col), BF16),
            pltpu.VMEM((chunks, 2, 4, 3, q1, col), BF16),
            pltpu.VMEM((chunks, 4, 4, 3, q2, col), BF16),
            pltpu.VMEM((chunks, 2, 2, 3, q2, col), BF16),
            pltpu.VMEM((chunks, 2, 4, 3, q2, col), BF16),
            pltpu.VMEM((chunks, 2, 4, 4, 2, 3, q2, col), BF16),
            pltpu.VMEM((chunks, experts // chunks, packed, LANES), BF16),
            pltpu.VMEM((experts, packed, LANES), BF16),
            pltpu.VMEM((experts * cap, toks), BF16),
            pltpu.VMEM((4 * LANES, toks), BF16),
            pltpu.VMEM((2 * LANES, hid), BF16),
            pltpu.VMEM((2 * LANES, hid), BF16),
            pltpu.VMEM((2 * LANES, hid), BF16),
            pltpu.VMEM((chunks, rows, 2 * LANES), BF16),
            pltpu.VMEM((chunks, rows, 2 * LANES), BF16),
            *[pltpu.VMEM(shape.shape, BF16) for shape in shapes],
            dma((5,)),
            dma((5,)),
            dma,
            dma((chunks,)),
            dma,
            dma((chunks,)),
            dma((chunks, 4)),
            dma((chunks, 2, 2)),
            dma((chunks, 2)),
            dma((chunks, 2, 2)),
            dma((chunks, 2)),
            dma((chunks, 2, 3)),
            dma((chunks, 2, 3)),
        ],
        compiler_params=pltpu.CompilerParams(
            collective_id=0, has_side_effects=True, vmem_limit_bytes=60 * 1024 * 1024
        ),
    )(tokens.T, grad_out.T, expert_ids.T, gates.T, w_gate[0], w_up[0], w_down[0].T)
    mixed, grad_tokens, grad_gate, grad_up, grad_down = pl.pallas_call(
        deliver,
        out_shape=shapes,
        in_specs=[anywhere] * 5,
        out_specs=(anywhere,) * 5,
        scratch_shapes=[pltpu.VMEM(shape.shape, BF16) for shape in shapes] + [dma((5,)), dma((5,))],
    )(*results)
    return (mixed.T, grad_tokens.T, grad_gate[None], grad_up[None], grad_down.T[None])


def solution(mesh):
    placed = (
        P("expert", "dp"),
        P("expert", "dp"),
        P("expert", None),
        P("expert", None),
        P("expert", "dp", None),
        P("expert", "dp", None),
        P("expert", None, "dp"),
    )
    return jax.shard_map(
        body,
        mesh=mesh,
        in_specs=placed,
        out_specs=(
            P("expert", "dp"),
            P("expert", "dp"),
            P("expert", "dp", None),
            P("expert", "dp", None),
            P("expert", None, "dp"),
        ),
        check_vma=False,
    )
```
